32 devices in a mesh: groups: 2 (over y), shot: 4 (over z), slab: 4 (over x, core).
Axes of the slice: x: 2, y: 2, z: 4, core: 2. Of those that a mesh axis runs over, the one named last changes fastest.
Arguments:
- model: float32 [64, 64, 128], P(('groups', 'slab')), parts along dimension 0, may hold values from 0.05 to 0.3
- fwd_now: float32 [8, 32, 64, 128], P(('groups', 'shot'), 'slab'), parts along dimension 0, may hold values from -6 to 6
- fwd_next: float32 [8, 32, 64, 128], P(('groups', 'shot'), 'slab'), parts along dimension 0, may hold values from -6 to 6
- adj_now: float32 [8, 32, 64, 128], P(('groups', 'shot'), 'slab'), parts along dimension 0, may hold values from -6 to 6
- adj_next: float32 [8, 32, 64, 128], P(('groups', 'shot'), 'slab'), parts along dimension 0, may hold values from -6 to 6
- wavelet: float32 [8, 8], P(('groups', 'shot')), parts along dimension 0, may hold values from -16 to 16
- misfit: float32 [8, 8, 128], P(('groups', 'shot')), parts along dimension 0, may hold values from -6 to 6
- src_index: int32 [8], P(('groups', 'shot')), parts along dimension 0, may hold values from 0 to 262143
- rec_index: int32 [8, 128], P(('groups', 'shot')), parts along dimension 0, may hold values from 0 to 262143
Outputs:
- new_model: float32 [64, 64, 128], P(('groups', 'slab')), parts along dimension 0
- stepped: float32 [8, 32, 64, 128], P(('groups', 'shot'), 'slab'), parts along dimension 0
- adjoint_start: float32 [8, 32, 64, 128], P(('groups', 'shot'), 'slab'), parts along dimension 0
The draws below stay inside these ranges and needn't reach their ends.
There are 2 independent parts, one for each index of `groups`. The reference program is written for one: setup_inputs(seed, part) draws one part's arguments, and reference() takes and returns one part's arrays. A program takes and returns all parts, laid end to end along the dimension named above; each array names one. Nothing has to cross between parts.
All inputs are finite; a program needn't handle non-finite values. Where the reference program divides by a largest or mean magnitude, that divisor is 1e-20 or more.
Results may differ from the reference program's by a relative error of at most 0.00002.
Values sent between devices are 32-bit elements; how exact they have to be, the bound alone decides.
No kernel may reach another device: no remote copies, remote signals or barrier semaphores. Data moves between devices by JAX's collectives and lax.ppermute only.
A program may use at most 64 MiB of HBM per device.

```python
import jax
import jax.numpy as jnp

NY = 64
NZ = 128
ITERS = 8
NREC = 128
NX = 32
NSHOT = 4


def set_ends(values, key, low, top_value):
    longest = values.shape.index(max(values.shape))
    spots = []
    for shift in (0, 1):
        where = [jax.random.randint(jax.random.fold_in(key, axis), (), 0, length) for axis, length in enumerate(values.shape)]
        where[longest] = (where[longest] + shift) % values.shape[longest]
        spots.append(tuple(where))
    return values.at[spots[0]].set(low).at[spots[1]].set(top_value)


def block_scale(rng, shape, split, smallest, largest):
    def one(dim, shards_of):
        heights = jax.random.uniform(jax.random.fold_in(jax.random.fold_in(rng, 6), dim), (shards_of,), jnp.float32, smallest / len(split), largest / len(split))
        return jnp.repeat(jnp.exp(heights), shape[dim] // shards_of).reshape((-1,) + (1,) * (len(shape) - dim - 1))

    level = one(*split[0])
    for cut in split[1:]:
        level = level * one(*cut)
    return level


def normal_values(key, shape, deviation, bound, split=(), kind=jnp.bfloat16):
    values = deviation * jax.random.normal(key, shape, jnp.float32)
    if split:
        values = values * block_scale(key, shape, split, -0.22, 0.18)
    return jnp.clip(values, -bound, bound).astype(kind)


def setup_inputs(seed: int = 0, part: int = 0) -> dict:
    key_list = jax.random.split(jax.random.key(seed), 10)
    part_keys = jax.random.split(jax.random.fold_in(key_list[9], part), 10)
    return {
        "model": jnp.clip(0.05 + 0.25 * jax.random.uniform(part_keys[0], (NX, NY, NZ), jnp.float32) ** block_scale(part_keys[0], (NX, NY, NZ), ((0, 4),), -0.2, 0.2), 0.05, 0.3),
        "fwd_now": normal_values(part_keys[1], (NSHOT, NX, NY, NZ), 1.0, 6.0, ((0, 4), (1, 4)), jnp.float32),
        "fwd_next": normal_values(part_keys[2], (NSHOT, NX, NY, NZ), 1.0, 6.0, ((0, 4), (1, 4)), jnp.float32),
        "adj_now": normal_values(part_keys[3], (NSHOT, NX, NY, NZ), 1.0, 6.0, ((0, 4), (1, 4)), jnp.float32),
        "adj_next": normal_values(part_keys[4], (NSHOT, NX, NY, NZ), 1.0, 6.0, ((0, 4), (1, 4)), jnp.float32),
        "wavelet": normal_values(part_keys[5], (NSHOT, ITERS), 4.0, 16.0, ((0, 4),), jnp.float32),
        "misfit": normal_values(part_keys[6], (NSHOT, ITERS, NREC), 1.0, 6.0, ((0, 4),), jnp.float32),
        "src_index": set_ends(jax.random.randint(part_keys[7], (NSHOT,), 0, NX * NY * NZ), jax.random.fold_in(part_keys[7], 1), 0, (NX * NY * NZ) - 1).astype(jnp.int32),
        "rec_index": set_ends(jax.random.randint(part_keys[8], (NSHOT, NREC), 0, NX * NY * NZ), jax.random.fold_in(part_keys[8], 1), 0, (NX * NY * NZ) - 1).astype(jnp.int32),
    }


def laplace(field):
    padded = jnp.pad(field, ((0, 0), (1, 1), (1, 1), (1, 1)))
    beside = padded[:, 2:, 1:-1, 1:-1] + padded[:, :-2, 1:-1, 1:-1]
    beside = beside + padded[:, 1:-1, 2:, 1:-1] + padded[:, 1:-1, :-2, 1:-1]
    beside = beside + padded[:, 1:-1, 1:-1, 2:] + padded[:, 1:-1, 1:-1, :-2]
    return beside - 6.0 * field


def inject(field, index, values):
    shots = field.shape[0]
    flat = field.reshape(shots, -1)
    rows = jnp.arange(shots, dtype=jnp.int32).reshape((shots,) + (1,) * (index.ndim - 1))
    rows = jnp.broadcast_to(rows, index.shape)
    flat = flat.at[rows, index].add(values)
    return flat.reshape(field.shape)


def reference(model, fwd_now, fwd_next, adj_now, adj_next, wavelet, misfit, src_index, rec_index):
    wave, wave_later = fwd_now, fwd_next
    adjoint, adjoint_later = adj_now, adj_next
    image = jnp.zeros_like(fwd_now)
    for step in range(ITERS):
        lap_wave = laplace(wave)
        lap_adjoint = laplace(adjoint)
        image = image + adjoint * lap_wave
        wave_prior = 2.0 * wave - wave_later + model[None] * lap_wave
        wave_prior = inject(wave_prior, src_index, wavelet[:, step])
        adjoint_prior = 2.0 * adjoint - adjoint_later + model[None] * lap_adjoint
        adjoint_prior = inject(adjoint_prior, rec_index, misfit[:, step, :])
        wave_later, wave = wave, wave_prior
        adjoint_later, adjoint = adjoint, adjoint_prior
    gradient = jnp.sum(image, axis=0)
    peak = jnp.max(jnp.abs(gradient))
    new_model = jnp.clip(model - 0.1 * gradient / (peak + 1e-6), 0.05, 0.3)
    stepped = 2.0 * wave - wave_later + new_model[None] * laplace(wave)
    return new_model, stepped, adjoint
```

```python
import functools

import jax
import jax.numpy as jnp
from jax import lax
from jax.experimental import pallas as pl
from jax.experimental.pallas import tpu as pltpu
from jax.sharding import PartitionSpec as P

ITERS = 8
GUARD = 8
LANES = 128
VMEM = pltpu.VMEM
SMEM = pltpu.SMEM
HBM = pl.ANY


def pairs(count, start):
    low = [(i, i + 1) for i in range(start, count - 1, 2)]
    return low + [(b, a) for a, b in low]


def partner_perms(count):
    if count & (count - 1) == 0:
        return [[(i, i ^ m) for i in range(count)] for m in range(1, count)]
    return [[(i, (i + m) % count) for i in range(count)] for m in range(1, count)]


def send_slot(me, m, count):
    return me ^ m if count & (count - 1) == 0 else lax.rem(me + m, count)


def from_slot(me, m, count):
    return me ^ m if count & (count - 1) == 0 else lax.rem(me - m + count, count)


def spec(space):
    return pl.BlockSpec(memory_space=space)


def cost(flops, nbytes):
    return pl.CostEstimate(flops=int(flops), bytes_accessed=int(nbytes), transcendentals=0)


def inject_kernel(depth, width, meta, rec_ref, misfit_ref, out_ref, left, right):
    rows = left.shape[0]
    index = rec_ref[...] - (meta[0] - depth) * (width * LANES)
    row_of = index // LANES
    row_of = jnp.where(index < 0, -1, row_of)
    lane_of = index - row_of * LANES
    group = 2 * width
    for first in range(0, rows, group):
        at = lax.broadcasted_iota(jnp.int32, (group, LANES), 0) + first
        hot = jnp.where(at == row_of, 1.0, 0.0).astype(jnp.bfloat16)
        for part in range(3):
            left[pl.ds(first, group), pl.ds(part * LANES, LANES)] = hot
    lane = lax.broadcasted_iota(jnp.int32, (LANES, LANES), 0)
    mine = lane == lane_of
    for k in range(ITERS):
        value = misfit_ref[pl.ds(k, 1), :]
        for part in range(3):
            piece = value.astype(jnp.bfloat16).astype(jnp.float32)
            value = value - piece
            right[pl.ds(k * LANES, LANES), pl.ds(part * LANES, LANES)] = jnp.where(
                mine, piece, 0.0
            ).astype(jnp.bfloat16)

    def pair(j, carry):
        cols = right[pl.ds(pl.multiple_of(j * 2 * LANES, 2 * LANES), 2 * LANES), :]
        both = lax.dot_general(
            left[...], cols, (((1,), (1,)), ((), ())), preferred_element_type=jnp.float32
        )
        out_ref[2 * j] = both[:, :LANES].reshape(out_ref.shape[1:])
        out_ref[2 * j + 1] = both[:, LANES:].reshape(out_ref.shape[1:])
        return carry

    lax.fori_loop(0, ITERS // 2, pair, 0)


def lap_block(src, p, r, first, last):
    c = src[p, pl.ds(r, 8), :]
    s = src[p + 1, pl.ds(r, 8), :] + src[p - 1, pl.ds(r, 8), :]
    s = s + src[p, pl.ds(r + 1, 8), :]
    s = s + src[p, pl.ds(r - 1, 8), :]
    s = s + jnp.where(last, 0.0, pltpu.roll(c, LANES - 1, 1))
    s = s + jnp.where(first, 0.0, pltpu.roll(c, 1, 1))
    return c, s - 6.0 * c


def load_field(depth, width, even, now, later, a_in, b_in, at_now, at_later, cur, old, sem):
    rows = pl.ds(GUARD, width)
    out = []

    def own(src, dst, i):
        c = pltpu.make_async_copy(src, dst.at[pl.ds(depth, depth), rows], sem.at[i])
        c.start()
        out.append(c)

    own(now, cur, 0)
    own(later, old, 1)

    def halo(low, high, i):
        n = depth - 1
        for j, (src, dst, off, size, where) in enumerate(
            (
                (low, cur, at_now, depth, 0),
                (low, old, at_later, n, 1),
                (high, cur, at_now, depth, 2 * depth),
                (high, old, at_later, n, 2 * depth),
            )
        ):
            pltpu.make_async_copy(
                src.at[pl.ds(off, size)], dst.at[pl.ds(where, size), rows], sem.at[i + j]
            ).start()

    @pl.when(even)
    def _():
        halo(b_in, a_in, 2)

    @pl.when(jnp.logical_not(even))
    def _():
        halo(a_in, b_in, 2)

    n = depth - 1
    for j, (dst, size, where) in enumerate(
        ((cur, depth, 0), (old, n, 1), (cur, depth, 2 * depth), (old, n, 2 * depth))
    ):
        out.append(
            pltpu.make_async_copy(
                a_in.at[pl.ds(0, size)], dst.at[pl.ds(where, size), rows], sem.at[2 + j]
            )
        )
    return out


def load_model(depth, even, model, a_in, b_in, at, mod, sem):
    n = depth - 1
    own = pltpu.make_async_copy(model, mod.at[pl.ds(depth, depth)], sem.at[6])
    own.start()

    def halo(low, high):
        pltpu.make_async_copy(low.at[pl.ds(at, n)], mod.at[pl.ds(1, n)], sem.at[7]).start()
        pltpu.make_async_copy(high.at[pl.ds(at, n)], mod.at[pl.ds(2 * depth, n)], sem.at[8]).start()

    @pl.when(even)
    def _():
        halo(b_in, a_in)

    @pl.when(jnp.logical_not(even))
    def _():
        halo(a_in, b_in)

    return [
        own,
        pltpu.make_async_copy(a_in.at[pl.ds(at, n)], mod.at[pl.ds(1, n)], sem.at[7]),
        pltpu.make_async_copy(a_in.at[pl.ds(at, n)], mod.at[pl.ds(2 * depth, n)], sem.at[8]),
    ]


def clear_guards(field):
    planes, rows, _ = field.shape

    def one(p, carry):
        field[p, pl.ds(0, GUARD), :] = jnp.zeros((GUARD, LANES), jnp.float32)
        field[p, pl.ds(rows - GUARD, GUARD), :] = jnp.zeros((GUARD, LANES), jnp.float32)
        return carry

    lax.fori_loop(0, planes, one, 0)


def forward_kernel(
    depth, width, meta, wavelet, src_index, model, now, later, a_in, b_in,
    last_out, base_out, lap_out, a_edge, b_edge,
    cur, old, mod, sem,
):
    even = meta[1] == 0
    waits = load_field(depth, width, even, now, later, a_in, b_in, 0, depth, cur, old, sem)
    waits += load_model(depth, even, model, a_in, b_in, 2 * depth - 1, mod, sem)
    clear_guards(cur)
    clear_guards(old)
    for w in waits:
        w.wait()
    lane = lax.broadcasted_iota(jnp.int32, (8, LANES), 1)
    first, last = lane == 0, lane == LANES - 1
    source = src_index[0] - (meta[0] - depth) * (width * LANES)
    src_row = jnp.maximum(source, 0) // LANES
    src_plane = jnp.where(source < 0, -1, src_row // width)
    src_y = lax.rem(src_row, width)
    src_lane = lax.rem(jnp.maximum(source, 0), LANES)
    bufs = (cur, old)
    for k in range(ITERS):
        s, d = bufs[k % 2], bufs[(k + 1) % 2]

        def plane(p, carry, keep):
            for r in range(0, width, 8):
                c, lap = lap_block(s, p, GUARD + r, first, last)
                here = (p, pl.ds(GUARD + r, 8), slice(None))
                d[here] = 2.0 * c - d[here] + mod[p, pl.ds(r, 8), :] * lap
                if keep:
                    lap_out[k, p - depth, pl.ds(r, 8), :] = lap
            return carry

        low, high = k + 1, 3 * depth - 1 - k
        lax.fori_loop(low, depth, functools.partial(plane, keep=False), 0)
        lax.fori_loop(depth, 2 * depth, functools.partial(plane, keep=True), 0)
        lax.fori_loop(2 * depth, high, functools.partial(plane, keep=False), 0)

        @pl.when((src_plane >= low) & (src_plane < high))
        def _():
            here = (src_plane, pl.ds(GUARD + src_y, 1), slice(None))
            at = lax.broadcasted_iota(jnp.int32, (1, LANES), 1) == src_lane
            d[here] = d[here] + jnp.where(at, wavelet[0, k], 0.0)

    u, u_later = bufs[ITERS % 2], bufs[(ITERS + 1) % 2]
    rows = pl.ds(GUARD, width)

    def finish(p, carry):
        c = u[depth + p, rows, :]
        last_out[p] = c
        base_out[p] = 2.0 * c - u_later[depth + p, rows, :]
        return carry

    lax.fori_loop(0, depth, finish, 0)
    a_edge[0] = u[jnp.where(even, 2 * depth - 1, depth), rows, :]
    b_edge[0] = u[jnp.where(even, depth, 2 * depth - 1), rows, :]


def adjoint_kernel(
    depth, width, shots, meta, model, now, later, fa_in, fb_in, a_in, b_in, laps, extra,
    last_out, *rest,
):
    pieces = rest[:shots]
    image, cur, old, mod, sem = rest[shots:]
    even = meta[1] == 0
    waits = load_field(depth, width, even, now, later, a_in, b_in, 0, depth, cur, old, sem)
    waits += load_model(depth, even, model, fa_in, fb_in, 2 * depth - 1, mod, sem)
    clear_guards(cur)
    clear_guards(old)
    for w in waits:
        w.wait()
    lane = lax.broadcasted_iota(jnp.int32, (8, LANES), 1)
    first, last = lane == 0, lane == LANES - 1
    bufs = (cur, old)
    for k in range(ITERS):
        s, d = bufs[k % 2], bufs[(k + 1) % 2]

        def plane(p, carry, keep):
            for r in range(0, width, 8):
                c, lap = lap_block(s, p, GUARD + r, first, last)
                here = (p, pl.ds(GUARD + r, 8), slice(None))
                rows = pl.ds(r, 8)
                new = 2.0 * c - d[here] + mod[p, rows, :] * lap
                d[here] = new + extra[k, p, rows, :]
                if keep:
                    q = p - depth
                    add = c * laps[k, q, rows, :]
                    into = pl.ds(pl.multiple_of(q * width + r, 8), 8)
                    image[into, :] = add if k == 0 else image[into, :] + add
            return carry

        low, high = k + 1, 3 * depth - 1 - k
        lax.fori_loop(low, depth, functools.partial(plane, keep=False), 0)
        lax.fori_loop(depth, 2 * depth, functools.partial(plane, keep=True), 0)
        lax.fori_loop(2 * depth, high, functools.partial(plane, keep=False), 0)

    a = bufs[ITERS % 2]

    def finish(p, carry):
        last_out[p] = a[depth + p, pl.ds(GUARD, width), :]
        return carry

    lax.fori_loop(0, depth, finish, 0)
    n = depth * width // shots
    for m in range(shots):
        to = meta[2] if m == 0 else send_slot(meta[2], m, shots)
        pieces[m][...] = image[pl.ds(pl.multiple_of(to * n, n), n), :]


def sum_kernel(*refs):
    *parts, grad, top = refs
    total = parts[0][...]
    for part in parts[1:]:
        total = total + part[...]
    grad[...] = total
    top[...] = jnp.broadcast_to(jnp.max(jnp.abs(total)), top.shape)


def final_kernel(depth, width, shots, meta, *refs):
    n = depth * width // shots
    grads = refs[:shots]
    tops, model, u, base, a_edge, b_edge, new_model, stepped, pad, grad = refs[shots:]
    even = meta[1] == 0
    rows = pl.ds(GUARD, width)
    clear_guards(pad)
    low, high = jnp.where(even, 0, depth + 1), jnp.where(even, depth + 1, 0)
    pad[low, rows, :] = b_edge[0]
    pad[high, rows, :] = a_edge[0]

    def place(p, carry):
        pad[p + 1, rows, :] = u[p]
        return carry

    lax.fori_loop(0, depth, place, 0)
    for m in range(shots):
        owner = meta[2] if m == 0 else from_slot(meta[2], m, shots)
        grad[pl.ds(pl.multiple_of(owner * n, n), n), :] = grads[m][...]
    peak = jnp.max(tops[...])
    lane = lax.broadcasted_iota(jnp.int32, (8, LANES), 1)
    first, last = lane == 0, lane == LANES - 1

    def plane(p, carry):
        for r in range(0, width, 8):
            g = grad[pl.ds(pl.multiple_of(p * width + r, 8), 8), :]
            new = jnp.clip(model[p, pl.ds(r, 8), :] - 0.1 * g / (peak + 1e-06), 0.05, 0.3)
            new_model[p, pl.ds(r, 8), :] = new
            _, lap = lap_block(pad, p + 1, GUARD + r, first, last)
            stepped[p, pl.ds(r, 8), :] = base[p, pl.ds(r, 8), :] + new * lap
        return carry

    lax.fori_loop(0, depth, plane, 0)


def per_device(model, fwd_now, fwd_next, adj_now, adj_next, wavelet, misfit, src_index, rec_index):
    f32 = jnp.float32
    depth, width, length = model.shape
    assert length == LANES and fwd_now.shape[0] == 1 and width % 8 == 0
    u0, u1, a0, a1 = fwd_now[0], fwd_next[0], adj_now[0], adj_next[0]
    slabs, shots = lax.axis_size("slab"), lax.axis_size("shot")
    slab, shot = lax.axis_index("slab"), lax.axis_index("shot")
    parity = lax.rem(slab, 2)
    meta = jnp.stack([slab * depth, parity, shot]).astype(jnp.int32)
    perm_a, perm_b = pairs(slabs, 0), pairs(slabs, 1)

    def short(x, up):
        return lax.dynamic_slice_in_dim(x, up, depth - 1, 0)

    def packed(fields, up):
        return jnp.concatenate([fields[0]] + [short(x, up) for x in fields[1:]], axis=0)

    fb = lax.ppermute(packed((u0, u1, model), parity), "slab", perm_b)
    fa = lax.ppermute(packed((u0, u1, model), 1 - parity), "slab", perm_a)
    gb = lax.ppermute(packed((a0, a1), parity), "slab", perm_b)
    ga = lax.ppermute(packed((a0, a1), 1 - parity), "slab", perm_a)

    plane = (depth, width, LANES)
    planes = 3 * depth
    shape = jax.ShapeDtypeStruct
    extra = pl.pallas_call(
        functools.partial(inject_kernel, depth, width),
        out_shape=shape((ITERS, planes, width, LANES), f32),
        in_specs=[spec(SMEM), spec(VMEM), spec(VMEM)],
        out_specs=spec(VMEM),
        scratch_shapes=[
            VMEM((planes * width, 3 * LANES), jnp.bfloat16),
            VMEM((ITERS * LANES, 3 * LANES), jnp.bfloat16),
        ],
        cost_estimate=cost(2 * planes * width * 3 * LANES * ITERS * LANES, 4 * ITERS * planes * width * LANES),
        name="inject",
    )(meta, rec_index, misfit[0])

    def work():
        field = (planes, width + 2 * GUARD, LANES)
        return [VMEM(field, f32), VMEM(field, f32), VMEM((planes, width, LANES), f32), pltpu.SemaphoreType.DMA((9,))]

    cells = depth * width * LANES
    u, base, laps, a_edge, b_edge = pl.pallas_call(
        functools.partial(forward_kernel, depth, width),
        out_shape=[
            shape(plane, f32), shape(plane, f32), shape((ITERS, *plane), f32),
            shape((1, width, LANES), f32), shape((1, width, LANES), f32),
        ],
        in_specs=[spec(SMEM)] * 3 + [spec(HBM)] * 5,
        out_specs=[spec(VMEM)] * 5,
        scratch_shapes=work(),
        cost_estimate=cost(15 * ITERS * 2 * cells, 4 * cells * 20),
        name="forward",
    )(meta, wavelet, src_index, model, u0, u1, fa, fb)

    a_edge = lax.ppermute(a_edge, "slab", perm_a)
    b_edge = lax.ppermute(b_edge, "slab", perm_b)

    n = depth * width // shots
    a, *pieces = pl.pallas_call(
        functools.partial(adjoint_kernel, depth, width, shots),
        out_shape=[shape(plane, f32)] + [shape((n, LANES), f32)] * shots,
        in_specs=[spec(SMEM)] + [spec(HBM)] * 7 + [spec(VMEM)] * 2,
        out_specs=[spec(VMEM)] * (1 + shots),
        scratch_shapes=[VMEM((depth * width, LANES), f32), *work()],
        cost_estimate=cost(18 * ITERS * 2 * cells, 4 * cells * 40),
        name="adjoint",
    )(meta, model, a0, a1, fa, fb, ga, gb, laps, extra)

    perms = partner_perms(shots)
    parts = [pieces[0]] + [lax.ppermute(x, "shot", q) for x, q in zip(pieces[1:], perms)]
    grad, top = pl.pallas_call(
        sum_kernel,
        out_shape=[shape((n, LANES), f32), shape((8, LANES), f32)],
        in_specs=[spec(VMEM)] * shots,
        out_specs=[spec(VMEM)] * 2,
        cost_estimate=cost(shots * n * LANES, 4 * shots * n * LANES),
        name="total",
    )(*parts)
    grads = [grad] + [lax.ppermute(grad, "shot", q) for q in perms]
    tops = [top] + [lax.ppermute(top, "slab", q) for q in partner_perms(slabs)]
    top = functools.reduce(jnp.maximum, tops)
    tops = jnp.concatenate([top] + [lax.ppermute(top, "shot", q) for q in perms], axis=0)

    new_model, stepped = pl.pallas_call(
        functools.partial(final_kernel, depth, width, shots),
        out_shape=[shape(plane, f32), shape(plane, f32)],
        in_specs=[spec(SMEM)] + [spec(VMEM)] * (shots + 6),
        out_specs=[spec(VMEM)] * 2,
        scratch_shapes=[VMEM((depth + 2, width + 2 * GUARD, LANES), f32), VMEM((depth * width, LANES), f32)],
        cost_estimate=cost(20 * cells, 4 * 6 * cells),
        name="update",
    )(meta, *grads, tops, model, u, base, a_edge, b_edge)
    return new_model, stepped[None], a[None]


def solution(mesh):
    in_specs = (
        P(("groups", "slab"), None, None),
        P(("groups", "shot"), "slab", None, None),
        P(("groups", "shot"), "slab", None, None),
        P(("groups", "shot"), "slab", None, None),
        P(("groups", "shot"), "slab", None, None),
        P(("groups", "shot"), None),
        P(("groups", "shot"), None, None),
        P(("groups", "shot")),
        P(("groups", "shot"), None),
    )
    out_specs = (
        P(("groups", "slab"), None, None),
        P(("groups", "shot"), "slab", None, None),
        P(("groups", "shot"), "slab", None, None),
    )
    return jax.shard_map(
        per_device, mesh=mesh, in_specs=in_specs, out_specs=out_specs, check_vma=False
    )
```

```python
import functools

import jax
import jax.numpy as jnp
from jax import lax
from jax.experimental import pallas as pl
from jax.experimental.pallas import tpu as pltpu
from jax.sharding import PartitionSpec as P

ITERS = 8
GUARD = 8
LANES = 128
LIMIT = 16 * 2**20
VMEM = pltpu.VMEM
SMEM = pltpu.SMEM
HBM = pl.ANY


def pairs(count, start):
    low = [(i, i + 1) for i in range(start, count - 1, 2)]
    return low + [(b, a) for a, b in low]


def partner_perms(count):
    if count & (count - 1) == 0:
        return [[(i, i ^ m) for i in range(count)] for m in range(1, count)]
    return [[(i, (i + m) % count) for i in range(count)] for m in range(1, count)]


def send_slot(me, m, count):
    return me ^ m if count & (count - 1) == 0 else lax.rem(me + m, count)


def from_slot(me, m, count):
    return me ^ m if count & (count - 1) == 0 else lax.rem(me - m + count, count)


def spec(space):
    return pl.BlockSpec(memory_space=space)


def cost(flops, nbytes):
    return pl.CostEstimate(flops=int(flops), bytes_accessed=int(nbytes), transcendentals=0)


def pack_kernel(depth, short, *refs):
    fields, (to_a, to_b, sem) = refs[: 1 + short], refs[1 + short :]
    odd = lax.rem(lax.axis_index("slab"), 2)
    n = depth - 1

    def copies(up_a, up_b):
        out = []
        for j, (dst, up) in enumerate(((to_a, up_a), (to_b, up_b))):
            at = 0
            for i, field in enumerate(fields):
                size, skip = (depth, 0) if i == 0 else (n, up)
                out.append(
                    pltpu.make_async_copy(
                        field.at[pl.ds(skip, size)], dst.at[pl.ds(at, size)], sem.at[j, i]
                    )
                )
                at += size
        return out

    @pl.when(odd == 0)
    def _():
        for c in copies(1, 0):
            c.start()

    @pl.when(odd != 0)
    def _():
        for c in copies(0, 1):
            c.start()

    for c in copies(0, 0):
        c.wait()


def inject_kernel(depth, width, rec_ref, misfit_ref, out_ref, left, right):
    rows = left.shape[0]
    base = (lax.axis_index("slab") * depth - depth) * width
    index = rec_ref[...]
    row_of = index // LANES
    lane_of = index - row_of * LANES
    row_of = row_of - base
    group = 2 * width
    for first in range(0, rows, group):
        at = lax.broadcasted_iota(jnp.int32, (group, LANES), 0) + first
        hot = jnp.where(at == row_of, 1.0, 0.0).astype(jnp.bfloat16)
        for part in range(3):
            left[pl.ds(first, group), pl.ds(part * LANES, LANES)] = hot
    lane = lax.broadcasted_iota(jnp.int32, (LANES, LANES), 0)
    mine = lane == lane_of
    for k in range(ITERS):
        value = misfit_ref[pl.ds(k, 1), :]
        for part in range(3):
            piece = value.astype(jnp.bfloat16).astype(jnp.float32)
            value = value - piece
            right[pl.ds(k * LANES, LANES), pl.ds(part * LANES, LANES)] = jnp.where(
                mine, piece, 0.0
            ).astype(jnp.bfloat16)

    def pair(j, carry):
        cols = right[pl.ds(pl.multiple_of(j * 2 * LANES, 2 * LANES), 2 * LANES), :]
        both = lax.dot_general(
            left[...], cols, (((1,), (1,)), ((), ())), preferred_element_type=jnp.float32
        )
        out_ref[2 * j] = both[:, :LANES].reshape(out_ref.shape[1:])
        out_ref[2 * j + 1] = both[:, LANES:].reshape(out_ref.shape[1:])
        return carry

    lax.fori_loop(0, ITERS // 2, pair, 0)


def lap_block(src, p, r, first, last):
    c = src[p, pl.ds(r, 8), :]
    s = src[p + 1, pl.ds(r, 8), :] + src[p - 1, pl.ds(r, 8), :]
    s = s + src[p, pl.ds(r + 1, 8), :]
    s = s + src[p, pl.ds(r - 1, 8), :]
    s = s + jnp.where(last, 0.0, pltpu.roll(c, LANES - 1, 1))
    s = s + jnp.where(first, 0.0, pltpu.roll(c, 1, 1))
    return c, s - 6.0 * c


def edges():
    lane = lax.broadcasted_iota(jnp.int32, (8, LANES), 1)
    return lane == 0, lane == LANES - 1


def clear_guards(field):
    planes, rows, _ = field.shape
    zero = jnp.zeros((GUARD, LANES), jnp.float32)
    for p in range(planes):
        field[p, pl.ds(0, GUARD), :] = zero
        field[p, pl.ds(rows - GUARD, GUARD), :] = zero


def fill(depth, width, own, a_in, b_in, at, bufs, guard):
    rows = [pl.ds(GUARD if g else 0, width) for g in guard]

    def main(p, carry):
        for src, dst, r in zip(own, bufs, rows):
            dst[depth + 1 + p, r, :] = src[p]
        return carry

    lax.fori_loop(0, depth, main, 0)

    def sides(low, high):
        def one(p, carry):
            for start, whole, dst, r in zip(at[0], at[1], bufs, rows):
                if not whole:
                    dst[2 + p, r, :] = low[start[0]][start[1] + p]
                    dst[2 * depth + 1 + p, r, :] = high[start[0]][start[1] + p]
                else:
                    dst[1 + p, r, :] = low[start[0]][start[1] + p]
                    dst[2 * depth + 1 + p, r, :] = high[start[0]][start[1] + p]
            return carry

        lax.fori_loop(0, depth - 1, one, 0)
        for start, whole, dst, r in zip(at[0], at[1], bufs, rows):
            if whole:
                dst[depth, r, :] = low[start[0]][start[1] + depth - 1]
                dst[3 * depth, r, :] = high[start[0]][start[1] + depth - 1]

    even = lax.rem(lax.axis_index("slab"), 2) == 0

    @pl.when(even)
    def _():
        sides(b_in, a_in)

    @pl.when(jnp.logical_not(even))
    def _():
        sides(a_in, b_in)

    return even


def sweep(depth, k, body):
    outer = (depth - k) // 2

    def halo(j, carry):
        body((depth - 1 - 2 * j, depth - 2 - 2 * j, 2 * depth + 2 * j, 2 * depth + 1 + 2 * j), False)
        return carry

    lax.fori_loop(0, outer, halo, 0)
    assert depth % 4 == 0

    def inner(j, carry):
        body(tuple(depth + 4 * j + i for i in range(4)), True)
        return carry

    lax.fori_loop(0, depth // 4, inner, 0)


def forward_kernel(
    depth, width, wavelet, src_index, model, now, later, a_in, b_in,
    last_out, base_out, lap_out, a_edge, b_edge,
    cur, old, mod,
):
    clear_guards(cur)
    clear_guards(old)
    even = fill(
        depth, width, (now, later, model), (a_in,), (b_in,),
        (((0, 0), (0, depth), (0, 2 * depth - 1)), (True, False, False)),
        (cur, old, mod), (True, True, False),
    )
    first, last = edges()
    source = src_index[0]
    src_row = source // LANES
    src_lane = source - src_row * LANES
    src_row = src_row - (lax.axis_index("slab") * depth - depth) * width
    bufs = (cur, old)
    for k in range(ITERS):
        s, d = bufs[k % 2], bufs[(k + 1) % 2]

        def body(planes, keep):
            for p in planes:
                for r in range(0, width, 8):
                    c, lap = lap_block(s, p + 1, GUARD + r, first, last)
                    here = (p + 1, pl.ds(GUARD + r, 8), slice(None))
                    d[here] = 2.0 * c - d[here] + mod[p + 1, pl.ds(r, 8), :] * lap
                    if keep:
                        lap_out[k, p - depth, pl.ds(r, 8), :] = lap

        sweep(depth, k, body)

        @pl.when((src_row >= (k + 1) * width) & (src_row < (3 * depth - 1 - k) * width))
        def _():
            plane = src_row // width
            here = (plane + 1, pl.ds(GUARD + src_row - plane * width, 1), slice(None))
            at = lax.broadcasted_iota(jnp.int32, (1, LANES), 1) == src_lane
            d[here] = d[here] + jnp.where(at, wavelet[0, k], 0.0)

    u, u_later = bufs[ITERS % 2], bufs[(ITERS + 1) % 2]
    rows = pl.ds(GUARD, width)

    def finish(p, carry):
        c = u[depth + 1 + p, rows, :]
        last_out[p] = c
        base_out[p] = 2.0 * c - u_later[depth + 1 + p, rows, :]
        return carry

    lax.fori_loop(0, depth, finish, 0)
    a_edge[0] = u[jnp.where(even, 2 * depth, depth + 1), rows, :]
    b_edge[0] = u[jnp.where(even, depth + 1, 2 * depth), rows, :]


def adjoint_kernel(
    depth, width, shots, model, now, later, fa_in, fb_in, a_in, b_in, laps, extra,
    last_out, *rest,
):
    pieces = rest[:shots]
    image, cur, old, mod = rest[shots:]
    clear_guards(cur)
    clear_guards(old)
    fill(
        depth, width, (now, later, model), (a_in, fa_in), (b_in, fb_in),
        (((0, 0), (0, depth), (1, 2 * depth - 1)), (True, False, False)),
        (cur, old, mod), (True, True, False),
    )
    first, last = edges()
    bufs = (cur, old)
    for k in range(ITERS):
        s, d = bufs[k % 2], bufs[(k + 1) % 2]

        def body(planes, keep):
            for p in planes:
                for r in range(0, width, 8):
                    c, lap = lap_block(s, p + 1, GUARD + r, first, last)
                    here = (p + 1, pl.ds(GUARD + r, 8), slice(None))
                    rows = pl.ds(r, 8)
                    new = 2.0 * c - d[here] + mod[p + 1, rows, :] * lap
                    d[here] = new + extra[k, p, rows, :]
                    if keep:
                        q = p - depth
                        add = c * laps[k, q, rows, :]
                        into = pl.ds(pl.multiple_of(q * width + r, 8), 8)
                        image[into, :] = add if k == 0 else image[into, :] + add

        sweep(depth, k, body)

    a = bufs[ITERS % 2]

    def finish(p, carry):
        last_out[p] = a[depth + 1 + p, pl.ds(GUARD, width), :]
        return carry

    lax.fori_loop(0, depth, finish, 0)
    n = depth * width // shots
    me = lax.axis_index("shot")
    for m in range(shots):
        to = me if m == 0 else send_slot(me, m, shots)
        pieces[m][...] = image[pl.ds(pl.multiple_of(to * n, n), n), :]


def sum_kernel(*refs):
    *parts, out = refs
    n = parts[0].shape[0]
    top = jnp.zeros((8, LANES), jnp.float32)
    for r in range(0, n, 8):
        total = parts[0][pl.ds(r, 8), :]
        for part in parts[1:]:
            total = total + part[pl.ds(r, 8), :]
        out[pl.ds(r, 8), :] = total
        top = jnp.maximum(top, jnp.abs(total))
    out[pl.ds(n, 8), :] = top


def top_kernel(*refs):
    *parts, out = refs
    n = parts[0].shape[0] - 8
    top = parts[0][pl.ds(n, 8), :]
    for part in parts[1:]:
        top = jnp.maximum(top, part[pl.ds(n, 8), :])
    out[...] = top


def final_kernel(depth, width, shots, slabs, *refs):
    n = depth * width // shots
    grads, tops = refs[:shots], refs[shots : shots + slabs]
    model, u, base, a_edge, b_edge, new_model, stepped, pad, grad = refs[shots + slabs :]
    even = lax.rem(lax.axis_index("slab"), 2) == 0
    me = lax.axis_index("shot")
    rows = pl.ds(GUARD, width)
    clear_guards(pad)
    low, high = jnp.where(even, 0, depth + 1), jnp.where(even, depth + 1, 0)
    pad[low, rows, :] = b_edge[0]
    pad[high, rows, :] = a_edge[0]

    def place(p, carry):
        pad[p + 1, rows, :] = u[p]
        return carry

    lax.fori_loop(0, depth, place, 0)
    for m in range(shots):
        owner = me if m == 0 else from_slot(me, m, shots)
        grad[pl.ds(pl.multiple_of(owner * n, n), n), :] = grads[m][pl.ds(0, n), :]
    top = tops[0][...]
    for other in tops[1:]:
        top = jnp.maximum(top, other[...])
    peak = jnp.max(top)
    first, last = edges()

    def planes(j, carry):
        for i in range(4):
            p = 4 * j + i
            for r in range(0, width, 8):
                g = grad[pl.ds(pl.multiple_of(p * width + r, 8), 8), :]
                new = jnp.clip(model[p, pl.ds(r, 8), :] - 0.1 * g / (peak + 1e-06), 0.05, 0.3)
                new_model[p, pl.ds(r, 8), :] = new
                _, lap = lap_block(pad, p + 1, GUARD + r, first, last)
                stepped[p, pl.ds(r, 8), :] = base[p, pl.ds(r, 8), :] + new * lap
        return carry

    lax.fori_loop(0, depth // 4, planes, 0)


def on_chip(x):
    return pltpu.with_memory_space_constraint(x, VMEM)


def call(kernel, out_shape, args, spaces, scratch, flops, nbytes, name):
    args = [on_chip(x) if space is VMEM else x for x, space in zip(args, spaces)]
    return pl.pallas_call(
        kernel,
        out_shape=out_shape,
        in_specs=[spec(space) for space in spaces],
        out_specs=[spec(VMEM)] * len(out_shape),
        scratch_shapes=scratch,
        cost_estimate=cost(flops, nbytes),
        compiler_params=pltpu.CompilerParams(vmem_limit_bytes=LIMIT),
        name=name,
    )(*args)


def per_device(model, fwd_now, fwd_next, adj_now, adj_next, wavelet, misfit, src_index, rec_index):
    f32 = jnp.float32
    depth, width, length = model.shape
    assert length == LANES and fwd_now.shape[0] == 1 and width % 8 == 0
    u0, u1, a0, a1 = fwd_now[0], fwd_next[0], adj_now[0], adj_next[0]
    slabs, shots = lax.axis_size("slab"), lax.axis_size("shot")
    perm_a, perm_b = pairs(slabs, 0), pairs(slabs, 1)
    plane = (depth, width, LANES)
    planes = 3 * depth
    cells = depth * width * LANES
    shape = jax.ShapeDtypeStruct

    def packed(fields, name):
        size = depth + (len(fields) - 1) * (depth - 1)
        return call(
            functools.partial(pack_kernel, depth, len(fields) - 1),
            [VMEM((size, width, LANES), f32)] * 2,
            fields, [HBM] * len(fields), [pltpu.SemaphoreType.DMA((2, len(fields)))],
            0, 16 * len(fields) * cells, name,
        )

    fa, fb = packed((u0, u1, model), "pack_forward")
    fb = lax.ppermute(fb, "slab", perm_b)
    fa = lax.ppermute(fa, "slab", perm_a)
    ga, gb = packed((a0, a1), "pack_adjoint")
    gb = lax.ppermute(gb, "slab", perm_b)
    ga = lax.ppermute(ga, "slab", perm_a)

    (extra,) = call(
        functools.partial(inject_kernel, depth, width),
        [VMEM((ITERS, planes, width, LANES), f32)],
        (rec_index, misfit[0]), (VMEM, VMEM),
        [
            VMEM((planes * width, 3 * LANES), jnp.bfloat16),
            VMEM((ITERS * LANES, 3 * LANES), jnp.bfloat16),
        ],
        2 * planes * width * 3 * LANES * ITERS * LANES, 4 * ITERS * planes * width * LANES, "inject",
    )

    field = VMEM((planes + 2, width + 2 * GUARD, LANES), f32)
    work = [field, field, VMEM((planes + 2, width, LANES), f32)]
    edge = VMEM((1, width, LANES), f32)
    u, base, laps, a_edge, b_edge = call(
        functools.partial(forward_kernel, depth, width),
        [VMEM(plane, f32), VMEM(plane, f32), VMEM((ITERS, *plane), f32), edge, edge],
        (wavelet, src_index, model, u0, u1, fa, fb), [SMEM] * 2 + [VMEM] * 5,
        work, 15 * ITERS * 2 * cells, 4 * cells * 20, "forward",
    )

    a_edge = lax.ppermute(a_edge, "slab", perm_a)
    b_edge = lax.ppermute(b_edge, "slab", perm_b)

    n = depth * width // shots
    a, *pieces = call(
        functools.partial(adjoint_kernel, depth, width, shots),
        [shape(plane, f32)] + [VMEM((n, LANES), f32)] * shots,
        (model, a0, a1, fa, fb, ga, gb, laps, extra), [VMEM] * 9,
        [VMEM((depth * width, LANES), f32), *work],
        18 * ITERS * 2 * cells, 4 * cells * 40, "adjoint",
    )

    perms = partner_perms(shots)
    parts = [pieces[0]] + [lax.ppermute(x, "shot", q) for x, q in zip(pieces[1:], perms)]
    (grad,) = call(
        sum_kernel, [VMEM((n + 8, LANES), f32)], parts, [VMEM] * shots, [],
        shots * n * LANES, 4 * shots * n * LANES, "total",
    )
    grads = [grad] + [lax.ppermute(grad, "shot", q) for q in perms]
    (top,) = call(
        top_kernel, [VMEM((8, LANES), f32)], grads, [VMEM] * shots, [], 0, 4096 * shots, "top"
    )
    tops = [top] + [lax.ppermute(top, "slab", q) for q in partner_perms(slabs)]

    new_model, stepped = call(
        functools.partial(final_kernel, depth, width, shots, slabs),
        [shape(plane, f32), shape(plane, f32)],
        (*grads, *tops, model, u, base, a_edge, b_edge), [VMEM] * (shots + slabs + 5),
        [VMEM((depth + 2, width + 2 * GUARD, LANES), f32), VMEM((depth * width, LANES), f32)],
        20 * cells, 4 * 6 * cells, "update",
    )
    return new_model, stepped[None], a[None]


def solution(mesh):
    in_specs = (
        P(("groups", "slab"), None, None),
        P(("groups", "shot"), "slab", None, None),
        P(("groups", "shot"), "slab", None, None),
        P(("groups", "shot"), "slab", None, None),
        P(("groups", "shot"), "slab", None, None),
        P(("groups", "shot"), None),
        P(("groups", "shot"), None, None),
        P(("groups", "shot")),
        P(("groups", "shot"), None),
    )
    out_specs = (
        P(("groups", "slab"), None, None),
        P(("groups", "shot"), "slab", None, None),
        P(("groups", "shot"), "slab", None, None),
    )
    return jax.shard_map(
        per_device, mesh=mesh, in_specs=in_specs, out_specs=out_specs, check_vma=False
    )
```

```python
import functools

import jax
import jax.numpy as jnp
from jax import lax
from jax.experimental import pallas as pl
from jax.experimental.pallas import tpu as pltpu
from jax.sharding import PartitionSpec as P

ITERS = 8
REACH = 4
GUARD = 8
LANES = 128
LIMIT = 16 * 2**20
VMEM = pltpu.VMEM
SMEM = pltpu.SMEM
HBM = pl.ANY


def pairs(count, start):
    low = [(i, i + 1) for i in range(start, count - 1, 2)]
    return low + [(b, a) for a, b in low]


def partner_perms(count):
    if count & (count - 1) == 0:
        return {m: [(i, i ^ m) for i in range(count)] for m in range(1, count)}
    return {m: [(i, (i + m) % count) for i in range(count)] for m in range(1, count)}


def far_first(count):
    half = count // 2
    return [*range(half, count), *range(1, half)]


def send_slot(me, m, count):
    return me ^ m if count & (count - 1) == 0 else lax.rem(me + m, count)


def from_slot(me, m, count):
    return me ^ m if count & (count - 1) == 0 else lax.rem(me - m + count, count)


def spec(space):
    return pl.BlockSpec(memory_space=space)


def cost(flops, nbytes):
    return pl.CostEstimate(flops=int(flops), bytes_accessed=int(nbytes), transcendentals=0)


def is_even():
    return lax.rem(lax.axis_index("slab"), 2) == 0


def pack_kernel(depth, *refs):
    *fields, to_a, to_b, sem = refs

    def copies(up_a, up_b):
        out = []
        for j, (dst, up) in enumerate(((to_a, up_a), (to_b, up_b))):
            at = 0
            for i, field in enumerate(fields):
                size = REACH if i == 0 else REACH - 1
                out.append(
                    pltpu.make_async_copy(
                        field.at[pl.ds(depth - size if up else 0, size)],
                        dst.at[pl.ds(at, size)],
                        sem.at[j, i],
                    )
                )
                at += size
        return out

    even = is_even()

    @pl.when(even)
    def _():
        for c in copies(True, False):
            c.start()

    @pl.when(jnp.logical_not(even))
    def _():
        for c in copies(False, True):
            c.start()

    for c in copies(False, False):
        c.wait()


def inject_kernel(depth, width, rec_ref, misfit_ref, out_ref, left, right):
    rows = left.shape[0]
    base = (lax.axis_index("slab") * depth - REACH) * width
    index = rec_ref[...]
    row_of = index // LANES
    lane_of = index - row_of * LANES
    row_of = row_of - base
    group = 2 * width
    for first in range(0, rows, group):
        at = lax.broadcasted_iota(jnp.int32, (group, LANES), 0) + first
        hot = jnp.where(at == row_of, 1.0, 0.0).astype(jnp.bfloat16)
        for part in range(3):
            left[pl.ds(first, group), pl.ds(part * LANES, LANES)] = hot
    lane = lax.broadcasted_iota(jnp.int32, (LANES, LANES), 0)
    mine = lane == lane_of
    for k in range(ITERS):
        value = misfit_ref[pl.ds(k, 1), :]
        for part in range(3):
            piece = value.astype(jnp.bfloat16).astype(jnp.float32)
            value = value - piece
            right[pl.ds(k * LANES, LANES), pl.ds(part * LANES, LANES)] = jnp.where(
                mine, piece, 0.0
            ).astype(jnp.bfloat16)

    def pair(j, carry):
        cols = right[pl.ds(pl.multiple_of(j * 2 * LANES, 2 * LANES), 2 * LANES), :]
        both = lax.dot_general(
            left[...], cols, (((1,), (1,)), ((), ())), preferred_element_type=jnp.float32
        )
        out_ref[2 * j] = both[:, :LANES].reshape(out_ref.shape[1:])
        out_ref[2 * j + 1] = both[:, LANES:].reshape(out_ref.shape[1:])
        return carry

    lax.fori_loop(0, ITERS // 2, pair, 0)


def neighbours(src, p, r, first, last):
    c = src[p, pl.ds(r, 8), :]
    s = src[p + 1, pl.ds(r, 8), :] + src[p - 1, pl.ds(r, 8), :]
    s = s + src[p, pl.ds(r + 1, 8), :]
    s = s + src[p, pl.ds(r - 1, 8), :]
    s = s + jnp.where(last, 0.0, pltpu.roll(c, LANES - 1, 1))
    s = s + jnp.where(first, 0.0, pltpu.roll(c, 1, 1))
    return c, s


def edges():
    lane = lax.broadcasted_iota(jnp.int32, (8, LANES), 1)
    return lane == 0, lane == LANES - 1


def clear_guards(field):
    planes, rows, _ = field.shape
    zero = jnp.zeros((GUARD, LANES), jnp.float32)
    for p in range(planes):
        field[p, pl.ds(0, GUARD), :] = zero
        field[p, pl.ds(rows - GUARD, GUARD), :] = zero


def halo_sides(a_in, b_in, put):
    even = is_even()

    @pl.when(even)
    def _():
        put(b_in, a_in)

    @pl.when(jnp.logical_not(even))
    def _():
        put(a_in, b_in)


def fill(depth, width, now, later, cur, old):
    rows = pl.ds(GUARD, width)
    for p in range(depth):
        cur[REACH + p, rows, :] = now[p]
        old[REACH + p, rows, :] = later[p]

    def put(low, high):
        for p in range(REACH):
            cur[p, rows, :] = low[p]
            cur[REACH + depth + p, rows, :] = high[p]
        for p in range(REACH - 1):
            old[1 + p, rows, :] = low[REACH + p]
            old[REACH + depth + p, rows, :] = high[REACH + p]

    return put


def send(depth, width, u, u_later, to_a, to_b):
    even = is_even()
    rows = pl.ds(GUARD, width)
    for out, up in ((to_a, even), (to_b, jnp.logical_not(even))):
        for p in range(REACH):
            out[p] = u[jnp.where(up, depth, REACH) + p, rows, :]
        for p in range(REACH - 1):
            out[REACH + p] = u_later[jnp.where(up, depth + 1, REACH) + p, rows, :]


def blocks(depth, width, j):
    for p in range(j + 1, depth + 2 * REACH - 1 - j):
        for r in range(0, width, 8):
            yield p, r, REACH <= p < REACH + depth


def forward_kernel(depth, width, stage, *refs):
    wavelet, src_index, now, later, a_in, b_in = refs[:6]
    if stage == 0:
        model, u_out, later_out, lap_out, to_a, to_b, mod, weight, cur, old = refs[6:]
    else:
        mod, u_out, base_out, lap_out, to_a, to_b, cur, old = refs[6:]
    clear_guards(cur)
    clear_guards(old)
    put = fill(depth, width, now, later, cur, old)
    if stage == 0:
        n = REACH - 1

        def put_all(low, high):
            put(low, high)
            for p in range(n):
                mod[1 + p] = low[REACH + n + p]
                mod[REACH + depth + p] = high[REACH + n + p]

        halo_sides(a_in, b_in, put_all)
        for p in range(depth):
            mod[REACH + p] = model[p]
        for p in range(1, depth + 2 * REACH - 1):
            weight[p] = 2.0 - 6.0 * mod[p]
    else:
        halo_sides(a_in, b_in, put)
    first, last = edges()
    source = src_index[0]
    src_row = source // LANES
    src_lane = source - src_row * LANES
    src_row = src_row - (lax.axis_index("slab") * depth - REACH) * width
    bufs = (cur, old)
    for j in range(REACH):
        s, d = bufs[j % 2], bufs[(j + 1) % 2]
        for p, r, own in blocks(depth, width, j):
            c, around = neighbours(s, p, GUARD + r, first, last)
            lap = around - 6.0 * c
            here = (p, pl.ds(GUARD + r, 8), slice(None))
            d[here] = 2.0 * c - d[here] + mod[p, pl.ds(r, 8), :] * lap
            if own:
                lap_out[j, p - REACH, pl.ds(r, 8), :] = lap

        @pl.when((src_row >= (j + 1) * width) & (src_row < (depth + 2 * REACH - 1 - j) * width))
        def _():
            plane = src_row // width
            here = (plane, pl.ds(GUARD + src_row - plane * width, 1), slice(None))
            at = lax.broadcasted_iota(jnp.int32, (1, LANES), 1) == src_lane
            d[here] = d[here] + jnp.where(at, wavelet[0, stage * REACH + j], 0.0)

    u, u_later = bufs[REACH % 2], bufs[(REACH + 1) % 2]
    rows = pl.ds(GUARD, width)
    if stage == 0:
        send(depth, width, u, u_later, to_a, to_b)
        for p in range(depth):
            u_out[p] = u[REACH + p, rows, :]
            later_out[p] = u_later[REACH + p, rows, :]
    else:
        even = is_even()
        to_a[0] = u[jnp.where(even, REACH + depth - 1, REACH), rows, :]
        to_b[0] = u[jnp.where(even, REACH, REACH + depth - 1), rows, :]
        for p in range(depth):
            c = u[REACH + p, rows, :]
            u_out[p] = c
            base_out[p] = 2.0 * c - u_later[REACH + p, rows, :]


def adjoint_kernel(depth, width, shots, stage, *refs):
    now, later, a_in, b_in, mod, weight, laps, extra = refs[:8]
    if stage == 0:
        a_out, later_out, image, to_a, to_b, cur, old = refs[8:]
    else:
        so_far, a_out, *pieces, image, cur, old = refs[8:]
    clear_guards(cur)
    clear_guards(old)
    halo_sides(a_in, b_in, fill(depth, width, now, later, cur, old))
    first, last = edges()
    bufs = (cur, old)
    for j in range(REACH):
        s, d = bufs[j % 2], bufs[(j + 1) % 2]
        for p, r, own in blocks(depth, width, j):
            c, around = neighbours(s, p, GUARD + r, first, last)
            here = (p, pl.ds(GUARD + r, 8), slice(None))
            rows = pl.ds(r, 8)
            new = weight[p, rows, :] * c - d[here] + mod[p, rows, :] * around
            d[here] = new + extra[stage * REACH + j, p, rows, :]
            if own:
                q = p - REACH
                into = pl.ds(q * width + r, 8)
                add = c * laps[j, q, rows, :]
                if j > 0:
                    add = image[into, :] + add
                elif stage > 0:
                    add = so_far[into, :] + add
                image[into, :] = add

    a, a_later = bufs[REACH % 2], bufs[(REACH + 1) % 2]
    rows = pl.ds(GUARD, width)
    for p in range(depth):
        a_out[p] = a[REACH + p, rows, :]
    if stage == 0:
        send(depth, width, a, a_later, to_a, to_b)
        for p in range(depth):
            later_out[p] = a_later[REACH + p, rows, :]
    else:
        n = depth * width // shots
        me = lax.axis_index("shot")
        for m in range(shots):
            to = me if m == 0 else send_slot(me, m, shots)
            pieces[m][...] = image[pl.ds(pl.multiple_of(to * n, n), n), :]


def sum_kernel(*refs):
    *parts, out = refs
    n = parts[0].shape[0]
    top = jnp.zeros((8, LANES), jnp.float32)
    for r in range(0, n, 8):
        total = parts[0][pl.ds(r, 8), :]
        for part in parts[1:]:
            total = total + part[pl.ds(r, 8), :]
        out[pl.ds(r, 8), :] = total
        top = jnp.maximum(top, jnp.abs(total))
    out[pl.ds(n, 8), :] = top


def top_kernel(*refs):
    *parts, out = refs
    n = parts[0].shape[0] - 8
    top = parts[0][pl.ds(n, 8), :]
    for part in parts[1:]:
        top = jnp.maximum(top, part[pl.ds(n, 8), :])
    out[...] = top


def final_kernel(depth, width, shots, slabs, *refs):
    n = depth * width // shots
    grads, tops = refs[:shots], refs[shots : shots + slabs]
    model, u, base, a_edge, b_edge, new_model, stepped, pad, grad = refs[shots + slabs :]
    even = lax.rem(lax.axis_index("slab"), 2) == 0
    me = lax.axis_index("shot")
    rows = pl.ds(GUARD, width)
    clear_guards(pad)
    low, high = jnp.where(even, 0, depth + 1), jnp.where(even, depth + 1, 0)
    pad[low, rows, :] = b_edge[0]
    pad[high, rows, :] = a_edge[0]

    def place(p, carry):
        pad[p + 1, rows, :] = u[p]
        return carry

    lax.fori_loop(0, depth, place, 0)
    for m in range(shots):
        owner = me if m == 0 else from_slot(me, m, shots)
        grad[pl.ds(pl.multiple_of(owner * n, n), n), :] = grads[m][pl.ds(0, n), :]
    top = tops[0][...]
    for other in tops[1:]:
        top = jnp.maximum(top, other[...])
    peak = jnp.max(top)
    first, last = edges()

    def planes(j, carry):
        for i in range(4):
            p = 4 * j + i
            for r in range(0, width, 8):
                g = grad[pl.ds(pl.multiple_of(p * width + r, 8), 8), :]
                new = jnp.clip(model[p, pl.ds(r, 8), :] - 0.1 * g / (peak + 1e-06), 0.05, 0.3)
                new_model[p, pl.ds(r, 8), :] = new
                c, around = neighbours(pad, p + 1, GUARD + r, first, last)
                lap = around - 6.0 * c
                stepped[p, pl.ds(r, 8), :] = base[p, pl.ds(r, 8), :] + new * lap
        return carry

    lax.fori_loop(0, depth // 4, planes, 0)


def placed(x, space):
    if space is VMEM or space is pltpu.HBM:
        return pltpu.with_memory_space_constraint(x, space)
    return x


def call(kernel, outs, args, spaces, scratch, flops, nbytes, name):
    args = [placed(x, space) for x, space in zip(args, spaces)]
    return pl.pallas_call(
        kernel,
        out_shape=outs,
        in_specs=[spec(space) for space in spaces],
        out_specs=[spec(VMEM)] * len(outs),
        scratch_shapes=scratch,
        cost_estimate=cost(flops, nbytes),
        compiler_params=pltpu.CompilerParams(vmem_limit_bytes=LIMIT),
        name=name,
    )(*args)


def per_device(model, fwd_now, fwd_next, adj_now, adj_next, wavelet, misfit, src_index, rec_index):
    f32 = jnp.float32
    depth, width, length = model.shape
    assert length == LANES and fwd_now.shape[0] == 1 and width % 8 == 0 and depth >= REACH
    assert ITERS == 2 * REACH and REACH % 2 == 0
    u0, u1, a0, a1 = fwd_now[0], fwd_next[0], adj_now[0], adj_next[0]
    slabs, shots = lax.axis_size("slab"), lax.axis_size("shot")
    perm_a, perm_b = pairs(slabs, 0), pairs(slabs, 1)
    planes = depth + 2 * REACH
    cells = depth * width * LANES
    own = VMEM((depth, width, LANES), f32)
    wide = VMEM((planes, width, LANES), f32)
    field = VMEM((planes, width + 2 * GUARD, LANES), f32)
    halo = VMEM((2 * REACH - 1, width, LANES), f32)
    edge = VMEM((1, width, LANES), f32)
    laps = VMEM((REACH, depth, width, LANES), f32)
    out = jax.ShapeDtypeStruct((depth, width, LANES), f32)

    def exchange(to_a, to_b):
        b = lax.ppermute(to_b, "slab", perm_b)
        return lax.ppermute(to_a, "slab", perm_a), b

    def packed(fields, name):
        size = REACH + (len(fields) - 1) * (REACH - 1)
        return call(
            functools.partial(pack_kernel, depth),
            [VMEM((size, width, LANES), f32)] * 2,
            fields, [pltpu.HBM] * len(fields), [pltpu.SemaphoreType.DMA((2, len(fields)))],
            0, 4 * 4 * size * width * LANES, name,
        )

    def forward(stage, args, outs, name):
        return call(
            functools.partial(forward_kernel, depth, width, stage), outs, (wavelet, src_index, *args),
            [SMEM] * 2 + [VMEM] * len(args), [field] * 2, 15 * REACH * 2 * cells, 40 * cells, name,
        )

    def adjoint(stage, args, outs, scratch, name):
        return call(
            functools.partial(adjoint_kernel, depth, width, shots, stage), outs, args,
            [VMEM] * len(args), scratch + [field] * 2, 18 * REACH * 2 * cells, 40 * cells, name,
        )

    fa, fb = exchange(*packed((u0, u1, model), "pack_forward"))
    ga, gb = exchange(*packed((a0, a1), "pack_adjoint"))
    (extra,) = call(
        functools.partial(inject_kernel, depth, width),
        [VMEM((ITERS, planes, width, LANES), f32)],
        (rec_index, misfit[0]), (VMEM, VMEM),
        [
            VMEM((planes * width, 3 * LANES), jnp.bfloat16),
            VMEM((ITERS * LANES, 3 * LANES), jnp.bfloat16),
        ],
        2 * planes * width * 3 * LANES * ITERS * LANES, 4 * ITERS * planes * width * LANES, "inject",
    )

    u, u_later, lap, *to, mod, weight = forward(
        0, (u0, u1, fa, fb, model), [own, own, laps, halo, halo, wide, wide], "forward_first"
    )
    fa, fb = exchange(*to)
    image = VMEM((depth * width, LANES), f32)
    a, a_later, so_far, *to = adjoint(
        0, (a0, a1, ga, gb, mod, weight, lap, extra), [own, own, image, halo, halo], [], "adjoint_first"
    )
    ga, gb = exchange(*to)
    u, base, lap, *to = forward(
        1, (u, u_later, fa, fb, mod), [own, own, laps, edge, edge], "forward_second"
    )
    a_edge, b_edge = exchange(*to)
    n = depth * width // shots
    a, *pieces = adjoint(
        1, (a, a_later, ga, gb, mod, weight, lap, extra, so_far),
        [out] + [VMEM((n, LANES), f32)] * shots, [image], "adjoint_second",
    )

    perms = partner_perms(shots)
    order = far_first(shots)

    def with_others(own_one, pieces):
        got = {m: lax.ppermute(pieces[m], "shot", perms[m]) for m in order}
        return [own_one] + [got[m] for m in range(1, shots)]

    parts = with_others(pieces[0], pieces)
    (grad,) = call(
        sum_kernel, [VMEM((n + 8, LANES), f32)], parts, [VMEM] * shots, [],
        shots * n * LANES, 4 * shots * n * LANES, "total",
    )
    grads = with_others(grad, [grad] * shots)
    (top,) = call(
        top_kernel, [VMEM((8, LANES), f32)], grads, [VMEM] * shots, [], 0, 4096 * shots, "top"
    )
    tops = [top] + [lax.ppermute(top, "slab", q) for q in partner_perms(slabs).values()]

    new_model, stepped = call(
        functools.partial(final_kernel, depth, width, shots, slabs),
        [out, out],
        (*grads, *tops, model, u, base, a_edge, b_edge), [VMEM] * (shots + slabs + 5),
        [VMEM((depth + 2, width + 2 * GUARD, LANES), f32), VMEM((depth * width, LANES), f32)],
        20 * cells, 4 * 6 * cells, "update",
    )
    return new_model, stepped[None], a[None]


def solution(mesh):
    in_specs = (
        P(("groups", "slab"), None, None),
        P(("groups", "shot"), "slab", None, None),
        P(("groups", "shot"), "slab", None, None),
        P(("groups", "shot"), "slab", None, None),
        P(("groups", "shot"), "slab", None, None),
        P(("groups", "shot"), None),
        P(("groups", "shot"), None, None),
        P(("groups", "shot")),
        P(("groups", "shot"), None),
    )
    out_specs = (
        P(("groups", "slab"), None, None),
        P(("groups", "shot"), "slab", None, None),
        P(("groups", "shot"), "slab", None, None),
    )
    return jax.shard_map(
        per_device, mesh=mesh, in_specs=in_specs, out_specs=out_specs, check_vma=False
    )
```

```python
import functools

import jax
import jax.numpy as jnp
from jax import lax
from jax.experimental import pallas as pl
from jax.experimental.pallas import tpu as pltpu
from jax.sharding import PartitionSpec as P

ITERS = 8
REACH = ITERS
GUARD = 8
LANES = 128
LIMIT = 16 * 2**20
VMEM = pltpu.VMEM
SMEM = pltpu.SMEM


def pairs(count, start):
    low = [(i, i + 1) for i in range(start, count - 1, 2)]
    return low + [(b, a) for a, b in low]


def partner_perms(count):
    if count & (count - 1) == 0:
        return {m: [(i, i ^ m) for i in range(count)] for m in range(1, count)}
    return {m: [(i, (i + m) % count) for i in range(count)] for m in range(1, count)}


def far_first(count):
    half = count // 2
    return [*range(half, count), *range(1, half)]


def send_slot(me, m, count):
    return me ^ m if count & (count - 1) == 0 else lax.rem(me + m, count)


def from_slot(me, m, count):
    return me ^ m if count & (count - 1) == 0 else lax.rem(me - m + count, count)


def spec(space):
    return pl.BlockSpec(memory_space=space)


def cost(flops, nbytes):
    return pl.CostEstimate(flops=int(flops), bytes_accessed=int(nbytes), transcendentals=0)


def is_even():
    return lax.rem(lax.axis_index("slab"), 2) == 0


def pack_kernel(depth, sizes, *refs):
    *fields, to_a, to_b, sem = refs

    def copies(up_a, up_b):
        out = []
        for j, (dst, up) in enumerate(((to_a, up_a), (to_b, up_b))):
            at = 0
            for i, (field, size) in enumerate(zip(fields, sizes)):
                out.append(
                    pltpu.make_async_copy(
                        field.at[pl.ds(depth - size if up else 0, size)],
                        dst.at[pl.ds(at, size)],
                        sem.at[j, i],
                    )
                )
                at += size
        return out

    even = is_even()

    @pl.when(even)
    def _():
        for c in copies(True, False):
            c.start()

    @pl.when(jnp.logical_not(even))
    def _():
        for c in copies(False, True):
            c.start()

    for c in copies(False, False):
        c.wait()


def inject_kernel(depth, width, rec_ref, misfit_ref, out_ref, left, right):
    rows = left.shape[0]
    base = (lax.axis_index("slab") * depth - REACH) * width
    index = rec_ref[...]
    row_of = index // LANES
    lane_of = index - row_of * LANES
    row_of = row_of - base
    group = 2 * width
    for first in range(0, rows, group):
        at = lax.broadcasted_iota(jnp.int32, (group, LANES), 0) + first
        hot = jnp.where(at == row_of, 1.0, 0.0).astype(jnp.bfloat16)
        for part in range(3):
            left[pl.ds(first, group), pl.ds(part * LANES, LANES)] = hot
    lane = lax.broadcasted_iota(jnp.int32, (LANES, LANES), 0)
    mine = lane == lane_of
    for k in range(ITERS):
        value = misfit_ref[pl.ds(k, 1), :]
        for part in range(3):
            piece = value.astype(jnp.bfloat16).astype(jnp.float32)
            value = value - piece
            right[pl.ds(k * LANES, LANES), pl.ds(part * LANES, LANES)] = jnp.where(
                mine, piece, 0.0
            ).astype(jnp.bfloat16)

    def pair(j, carry):
        cols = right[pl.ds(pl.multiple_of(j * 2 * LANES, 2 * LANES), 2 * LANES), :]
        both = lax.dot_general(
            left[...], cols, (((1,), (1,)), ((), ())), preferred_element_type=jnp.float32
        )
        out_ref[2 * j] = both[:, :LANES].reshape(out_ref.shape[1:])
        out_ref[2 * j + 1] = both[:, LANES:].reshape(out_ref.shape[1:])
        return carry

    lax.fori_loop(0, ITERS // 2, pair, 0)


def neighbours(src, p, r, first, last):
    c = src[p, pl.ds(r, 8), :]
    s = src[p + 1, pl.ds(r, 8), :] + src[p - 1, pl.ds(r, 8), :]
    s = s + src[p, pl.ds(r + 1, 8), :]
    s = s + src[p, pl.ds(r - 1, 8), :]
    s = s + jnp.where(last, 0.0, pltpu.roll(c, LANES - 1, 1))
    s = s + jnp.where(first, 0.0, pltpu.roll(c, 1, 1))
    return c, s


def edges():
    lane = lax.broadcasted_iota(jnp.int32, (8, LANES), 1)
    return lane == 0, lane == LANES - 1


def clear_guards(field):
    planes, rows, _ = field.shape
    zero = jnp.zeros((GUARD, LANES), jnp.float32)
    for p in range(planes):
        field[p, pl.ds(0, GUARD), :] = zero
        field[p, pl.ds(rows - GUARD, GUARD), :] = zero


def fill(depth, width, own, a_in, b_in, bufs):
    rows = [pl.ds(buf.shape[1] - width - GUARD if buf.shape[1] > width else 0, width) for buf in bufs]
    for src, buf, r in zip(own, bufs, rows):
        for p in range(depth):
            buf[REACH + p, r, :] = src[p]

    def put(low, high):
        for buf, r, (lo, at, size), (hi, _, _) in zip(bufs, rows, low, high):
            for p in range(size):
                buf[REACH - size + p, r, :] = lo[at + p]
                buf[REACH + depth + p, r, :] = hi[at + p]

    even = is_even()

    @pl.when(even)
    def _():
        put(b_in, a_in)

    @pl.when(jnp.logical_not(even))
    def _():
        put(a_in, b_in)


def blocks(depth, width, k):
    for p in range(k + 1, depth + 2 * REACH - 1 - k):
        for r in range(0, width, 8):
            yield p, r, REACH <= p < REACH + depth


def forward_kernel(
    depth, width, wavelet, src_index, now, later, model, ua_in, ub_in, ha_in, hb_in,
    u_out, base_out, lap_out, a_edge, b_edge, mod, weight,
    cur, old,
):
    n = REACH - 1
    clear_guards(cur)
    clear_guards(old)
    fill(
        depth, width, (now, later, model),
        ((ua_in, 0, REACH), (ha_in, 0, n), (ha_in, n, n)),
        ((ub_in, 0, REACH), (hb_in, 0, n), (hb_in, n, n)),
        (cur, old, mod),
    )
    for p in range(1, depth + 2 * REACH - 1):
        weight[p] = 2.0 - 6.0 * mod[p]
    first, last = edges()
    source = src_index[0]
    src_row = source // LANES
    src_lane = source - src_row * LANES
    src_row = src_row - (lax.axis_index("slab") * depth - REACH) * width
    bufs = (cur, old)
    for k in range(ITERS):
        s, d = bufs[k % 2], bufs[(k + 1) % 2]
        for p, r, own in blocks(depth, width, k):
            c, around = neighbours(s, p, GUARD + r, first, last)
            lap = around - 6.0 * c
            here = (p, pl.ds(GUARD + r, 8), slice(None))
            d[here] = 2.0 * c - d[here] + mod[p, pl.ds(r, 8), :] * lap
            if own:
                lap_out[k, p - REACH, pl.ds(r, 8), :] = lap

        @pl.when((src_row >= (k + 1) * width) & (src_row < (depth + 2 * REACH - 1 - k) * width))
        def _():
            plane = src_row // width
            here = (plane, pl.ds(GUARD + src_row - plane * width, 1), slice(None))
            at = lax.broadcasted_iota(jnp.int32, (1, LANES), 1) == src_lane
            d[here] = d[here] + jnp.where(at, wavelet[0, k], 0.0)

    u, u_later = bufs[ITERS % 2], bufs[(ITERS + 1) % 2]
    rows = pl.ds(GUARD, width)
    even = is_even()
    a_edge[...] = u[jnp.where(even, REACH + depth - 1, REACH), rows, :]
    slab = lax.axis_index("slab")
    alone = jnp.where(even, slab == 0, slab == lax.axis_size("slab") - 1)
    b_edge[...] = jnp.where(alone, 0.0, u[jnp.where(even, REACH, REACH + depth - 1), rows, :])
    for p in range(depth):
        c = u[REACH + p, rows, :]
        u_out[p] = c
        base_out[p] = 2.0 * c - u_later[REACH + p, rows, :]


def adjoint_kernel(
    depth, width, shots, now, later, a_in, b_in, mod, weight, laps, extra, a_out, *rest
):
    *pieces, image, cur, old = rest
    n = REACH - 1
    clear_guards(cur)
    clear_guards(old)
    fill(
        depth, width, (now, later),
        ((a_in, 0, REACH), (a_in, REACH, n)), ((b_in, 0, REACH), (b_in, REACH, n)),
        (cur, old),
    )
    first, last = edges()
    bufs = (cur, old)
    for k in range(ITERS):
        s, d = bufs[k % 2], bufs[(k + 1) % 2]
        for p, r, own in blocks(depth, width, k):
            c, around = neighbours(s, p, GUARD + r, first, last)
            here = (p, pl.ds(GUARD + r, 8), slice(None))
            rows = pl.ds(r, 8)
            new = weight[p, rows, :] * c - d[here] + mod[p, rows, :] * around
            d[here] = new + extra[k, p, rows, :]
            if own:
                q = p - REACH
                into = pl.ds(q * width + r, 8)
                add = c * laps[k, q, rows, :]
                image[into, :] = image[into, :] + add if k > 0 else add

    a = bufs[ITERS % 2]
    for p in range(depth):
        a_out[p] = a[REACH + p, pl.ds(GUARD, width), :]
    n = depth * width // shots
    me = lax.axis_index("shot")
    for m in range(shots):
        to = me if m == 0 else send_slot(me, m, shots)
        pieces[m][...] = image[pl.ds(pl.multiple_of(to * n, n), n), :]


def sum_kernel(*refs):
    *parts, out = refs
    n = parts[0].shape[0]
    top = jnp.zeros((8, LANES), jnp.float32)
    for r in range(0, n, 8):
        total = parts[0][pl.ds(r, 8), :]
        for part in parts[1:]:
            total = total + part[pl.ds(r, 8), :]
        out[pl.ds(r, 8), :] = total
        top = jnp.maximum(top, jnp.abs(total))
    out[pl.ds(n, 8), :] = top


def top_kernel(shots, riders, *refs):
    parts, planes, outs = refs[:shots], refs[shots : shots + riders], refs[shots + riders :]
    n = parts[0].shape[0] - 8
    top = parts[0][pl.ds(n, 8), :]
    for part in parts[1:]:
        top = jnp.maximum(top, part[pl.ds(n, 8), :])
    outs[0][...] = top
    for plane, out in zip(planes, outs[1:]):
        rows = plane.shape[0]
        out[pl.ds(0, rows), :] = plane[...]
        out[pl.ds(rows, 8), :] = top


def final_kernel(depth, width, shots, tops, *refs):
    n = depth * width // shots
    grads, refs = refs[:shots], refs[shots:]
    tops, refs = refs[:tops], refs[tops:]
    model, u, base, a_edge, b_edge, new_model, stepped, pad, grad = refs
    even = is_even()
    me = lax.axis_index("shot")
    rows = pl.ds(GUARD, width)
    clear_guards(pad)
    low, high = jnp.where(even, 0, depth + 1), jnp.where(even, depth + 1, 0)
    pad[low, rows, :] = b_edge[pl.ds(0, width), :]
    pad[high, rows, :] = a_edge[pl.ds(0, width), :]
    for p in range(depth):
        pad[p + 1, rows, :] = u[p]
    for m in range(shots):
        owner = me if m == 0 else from_slot(me, m, shots)
        grad[pl.ds(pl.multiple_of(owner * n, n), n), :] = grads[m][pl.ds(0, n), :]
    top = tops[0][...]
    for other in tops[1:]:
        top = jnp.maximum(top, other[pl.ds(other.shape[0] - 8, 8), :])
    peak = jnp.max(top)
    first, last = edges()
    for p in range(depth):
        for r in range(0, width, 8):
            g = grad[pl.ds(p * width + r, 8), :]
            new = jnp.clip(model[p, pl.ds(r, 8), :] - 0.1 * g / (peak + 1e-06), 0.05, 0.3)
            new_model[p, pl.ds(r, 8), :] = new
            c, around = neighbours(pad, p + 1, GUARD + r, first, last)
            stepped[p, pl.ds(r, 8), :] = base[p, pl.ds(r, 8), :] + new * (around - 6.0 * c)


def placed(x, space):
    if space is VMEM or space is pltpu.HBM:
        return pltpu.with_memory_space_constraint(x, space)
    return x


def call(kernel, outs, args, spaces, scratch, flops, nbytes):
    args = [placed(x, space) for x, space in zip(args, spaces)]
    return pl.pallas_call(
        kernel,
        out_shape=outs,
        in_specs=[spec(space) for space in spaces],
        out_specs=[spec(VMEM)] * len(outs),
        scratch_shapes=scratch,
        cost_estimate=cost(flops, nbytes),
        compiler_params=pltpu.CompilerParams(vmem_limit_bytes=LIMIT),
    )(*args)


def per_device(model, fwd_now, fwd_next, adj_now, adj_next, wavelet, misfit, src_index, rec_index):
    f32 = jnp.float32
    depth, width, length = model.shape
    assert length == LANES and fwd_now.shape[0] == 1 and width % 8 == 0 and depth == REACH
    u0, u1, a0, a1 = fwd_now[0], fwd_next[0], adj_now[0], adj_next[0]
    slabs, shots = lax.axis_size("slab"), lax.axis_size("shot")
    perm_a, perm_b = pairs(slabs, 0), pairs(slabs, 1)
    planes = depth + 2 * REACH
    cells = depth * width * LANES
    own = VMEM((depth, width, LANES), f32)
    wide = VMEM((planes, width, LANES), f32)
    field = VMEM((planes, width + 2 * GUARD, LANES), f32)
    edge = VMEM((width, LANES), f32)
    out = jax.ShapeDtypeStruct((depth, width, LANES), f32)
    n = REACH - 1

    def exchange(to_a, to_b):
        b = lax.ppermute(to_b, "slab", perm_b)
        return lax.ppermute(to_a, "slab", perm_a), b

    def packed(fields, sizes):
        total = sum(sizes)
        return call(
            functools.partial(pack_kernel, depth, sizes),
            [VMEM((total, width, LANES), f32)] * 2,
            fields, [pltpu.HBM] * len(fields), [pltpu.SemaphoreType.DMA((2, len(fields)))],
            0, 4 * 4 * total * width * LANES,
        )

    ua, ub = exchange(u0, u0)
    ha, hb = exchange(*packed((u1, model), (n, n)))
    ga, gb = exchange(*packed((a0, a1), (REACH, n)))
    (extra,) = call(
        functools.partial(inject_kernel, depth, width),
        [VMEM((ITERS, planes, width, LANES), f32)],
        (rec_index, misfit[0]), (VMEM, VMEM),
        [
            VMEM((planes * width, 3 * LANES), jnp.bfloat16),
            VMEM((ITERS * LANES, 3 * LANES), jnp.bfloat16),
        ],
        2 * planes * width * 3 * LANES * ITERS * LANES, 4 * ITERS * planes * width * LANES,
    )

    u, base, laps, a_edge, b_edge, mod, weight = call(
        functools.partial(forward_kernel, depth, width),
        [own, own, VMEM((ITERS, depth, width, LANES), f32), edge, edge, wide, wide],
        (wavelet, src_index, u0, u1, model, ua, ub, ha, hb), [SMEM] * 2 + [VMEM] * 7,
        [field] * 2, 15 * ITERS * 2 * cells, 80 * cells,
    )
    rows = depth * width // shots
    a, *pieces = call(
        functools.partial(adjoint_kernel, depth, width, shots),
        [out] + [VMEM((rows, LANES), f32)] * shots,
        (a0, a1, ga, gb, mod, weight, laps, extra), [VMEM] * 8,
        [VMEM((depth * width, LANES), f32), field, field],
        18 * ITERS * 2 * cells, 80 * cells,
    )

    perms = partner_perms(shots)
    order = far_first(shots)

    def with_others(own_one, pieces):
        got = {}
        for m in order:
            got[m] = lax.ppermute(pieces[m], "shot", perms[m])
        return [own_one] + [got[m] for m in range(1, shots)]

    parts = with_others(pieces[0], pieces)
    (grad,) = call(
        sum_kernel, [VMEM((rows + 8, LANES), f32)], parts, [VMEM] * shots, [],
        shots * rows * LANES, 4 * shots * rows * LANES,
    )
    grads = with_others(grad, [grad] * shots)

    sides = {1: a_edge, 3: b_edge} if slabs == 4 else {}
    top, *ridden = call(
        functools.partial(top_kernel, shots, len(sides)),
        [VMEM((8, LANES), f32)] + [VMEM((width + 8, LANES), f32)] * len(sides),
        (*grads, *sides.values()), [VMEM] * (shots + len(sides)), [], 0, 4096 * shots,
    )
    riding = dict(zip(sides, ridden))
    got = {
        m: lax.ppermute(riding.get(m, top), "slab", q) for m, q in partner_perms(slabs).items()
    }
    if sides:
        a_edge, b_edge = got[1], got[3]
    else:
        a_edge, b_edge = exchange(a_edge, b_edge)
    tops = [top, *got.values()]

    new_model, stepped = call(
        functools.partial(final_kernel, depth, width, shots, len(tops)),
        [out, out],
        (*grads, *tops, model, u, base, a_edge, b_edge), [VMEM] * (shots + len(tops) + 5),
        [VMEM((depth + 2, width + 2 * GUARD, LANES), f32), VMEM((depth * width, LANES), f32)],
        20 * cells, 4 * 6 * cells,
    )
    return new_model, stepped[None], a[None]


def solution(mesh):
    in_specs = (
        P(("groups", "slab"), None, None),
        P(("groups", "shot"), "slab", None, None),
        P(("groups", "shot"), "slab", None, None),
        P(("groups", "shot"), "slab", None, None),
        P(("groups", "shot"), "slab", None, None),
        P(("groups", "shot"), None),
        P(("groups", "shot"), None, None),
        P(("groups", "shot")),
        P(("groups", "shot"), None),
    )
    out_specs = (
        P(("groups", "slab"), None, None),
        P(("groups", "shot"), "slab", None, None),
        P(("groups", "shot"), "slab", None, None),
    )
    return jax.shard_map(
        per_device, mesh=mesh, in_specs=in_specs, out_specs=out_specs, check_vma=False
    )
```

```python
import functools

import jax
import jax.numpy as jnp
from jax import lax
from jax.experimental import pallas as pl
from jax.experimental.pallas import tpu as pltpu
from jax.sharding import PartitionSpec as P

ITERS = 8
REACH = ITERS
GUARD = 8
LANES = 128
LIMIT = 16 * 2**20
VMEM = pltpu.VMEM
SMEM = pltpu.SMEM


def pairs(count, start):
    low = [(i, i + 1) for i in range(start, count - 1, 2)]
    return low + [(b, a) for a, b in low]


def partner_perms(count):
    if count & (count - 1) == 0:
        return {m: [(i, i ^ m) for i in range(count)] for m in range(1, count)}
    return {m: [(i, (i + m) % count) for i in range(count)] for m in range(1, count)}


def far_first(count):
    half = count // 2
    return [*range(half, count), *range(1, half)]


def send_slot(me, m, count):
    return me ^ m if count & (count - 1) == 0 else lax.rem(me + m, count)


def from_slot(me, m, count):
    return me ^ m if count & (count - 1) == 0 else lax.rem(me - m + count, count)


def spec(space):
    return pl.BlockSpec(memory_space=space)


def cost(flops, nbytes):
    return pl.CostEstimate(flops=int(flops), bytes_accessed=int(nbytes), transcendentals=0)


def is_even():
    return lax.rem(lax.axis_index("slab"), 2) == 0


def pack_kernel(depth, sizes, *refs):
    count = (len(refs) - 4) // 2
    args, (to_a, to_b), whole, (sem, own_sem) = (
        refs[:count], refs[count : count + 2], refs[count + 2 : -2], refs[-2:],
    )

    def copies(up_a, up_b):
        out = []
        for j, (dst, up) in enumerate(((to_a, up_a), (to_b, up_b))):
            at = 0
            for i, (field, size) in enumerate(zip(args, sizes)):
                out.append(
                    pltpu.make_async_copy(
                        field.at[pl.ds(depth - size if up else 0, size)],
                        dst.at[pl.ds(at, size)],
                        sem.at[j, i],
                    )
                )
                at += size
        return out

    even = is_even()

    @pl.when(even)
    def _():
        for c in copies(True, False):
            c.start()

    @pl.when(jnp.logical_not(even))
    def _():
        for c in copies(False, True):
            c.start()

    own = [
        pltpu.make_async_copy(src, dst, own_sem.at[i]) for i, (src, dst) in enumerate(zip(args, whole))
    ]
    for c in own:
        c.start()
    for c in copies(False, False) + own:
        c.wait()


def hot_rows(base, rec_ref, left):
    index = rec_ref[...]
    row_of = index // LANES
    lane_of = index - row_of * LANES
    row_of = row_of - base
    group = 128
    for first in range(0, left.shape[0], group):
        at = lax.broadcasted_iota(jnp.int32, (group, LANES), 0) + first
        hot = jnp.where(at == row_of, 1.0, 0.0).astype(jnp.bfloat16)
        for part in range(3):
            left[pl.ds(first, group), pl.ds(part * LANES, LANES)] = hot
    return lane_of


def residuals(left, first, size, lane_of, value):
    mine = lax.broadcasted_iota(jnp.int32, (LANES, LANES), 0) == lane_of
    parts = []
    for _ in range(3):
        piece = value.astype(jnp.bfloat16).astype(jnp.float32)
        value = value - piece
        parts.append(jnp.where(mine, piece, 0.0).astype(jnp.bfloat16))
    return lax.dot_general(
        left[pl.ds(first, size), :], jnp.concatenate(parts, axis=1),
        (((1,), (1,)), ((), ())), preferred_element_type=jnp.float32,
    )


def around(src, p, width, first, last):
    starts = range(GUARD, GUARD + width, 8)
    here = [src[p, pl.ds(r, 8), :] for r in starts]
    after = [pltpu.roll(c, LANES - 1, 1) for c in here]
    before = [pltpu.roll(c, 1, 1) for c in here]
    out = []
    for r, c, x, y in zip(starts, here, after, before):
        s = src[p + 1, pl.ds(r, 8), :] + src[p - 1, pl.ds(r, 8), :]
        s = s + src[p, pl.ds(r + 1, 8), :]
        s = s + src[p, pl.ds(r - 1, 8), :]
        s = s + jnp.where(last, 0.0, x)
        s = s + jnp.where(first, 0.0, y)
        out.append((r - GUARD, c, s))
    return out


def edges():
    lane = lax.broadcasted_iota(jnp.int32, (8, LANES), 1)
    return lane == 0, lane == LANES - 1


def clear_guards(field):
    planes, rows, _ = field.shape
    zero = jnp.zeros((GUARD, LANES), jnp.float32)
    for p in range(planes):
        field[p, pl.ds(0, GUARD), :] = zero
        field[p, pl.ds(rows - GUARD, GUARD), :] = zero


def fill(depth, width, reach, own, a_in, b_in, bufs):
    rows = [pl.ds(GUARD if buf.shape[1] > width else 0, width) for buf in bufs]
    for src, buf, r in zip(own, bufs, rows):
        for p in range(depth):
            buf[reach + p, r, :] = src[p]

    def put(low, high):
        for buf, r, (lo, at, size), (hi, _, _) in zip(bufs, rows, low, high):
            for p in range(size):
                buf[reach - size + p, r, :] = lo[at + p]
                buf[reach + depth + p, r, :] = hi[at + p]

    even = is_even()

    @pl.when(even)
    def _():
        put(b_in, a_in)

    @pl.when(jnp.logical_not(even))
    def _():
        put(a_in, b_in)


def forward_kernel(
    depth, width, wavelet, src_index, rec_index, misfit, now, later, model, ua_in, ub_in, ha_in, hb_in,
    u_out, later_out, lap_out, a_edge, b_edge, mod, weight, extra,
    amplitude, sem, left, cur, old,
):
    n = REACH - 1
    slab = lax.axis_index("slab")
    fetch = pltpu.make_async_copy(wavelet, amplitude, sem)
    fetch.start()
    clear_guards(cur)
    clear_guards(old)
    fill(
        depth, width, REACH, (now, later, model),
        ((ua_in, 0, REACH), (ha_in, 0, n), (ha_in, n, n)),
        ((ub_in, 0, REACH), (hb_in, 0, n), (hb_in, n, n)),
        (cur, old, mod),
    )
    lane_of = hot_rows((slab * depth - n) * width, rec_index, left)
    fetch.wait()
    for p in range(1, depth + 2 * REACH - 1):
        weight[p] = 2.0 - 6.0 * mod[p]
    first, last = edges()
    source = src_index[0]
    src_row = source // LANES
    src_lane = source - src_row * LANES
    src_row = src_row - (slab * depth - REACH) * width
    bufs = (cur, old)
    for k in range(ITERS):
        s, d = bufs[k % 2], bufs[(k + 1) % 2]
        low, high = (k + 1, depth + 2 * n - 1 - k) if k < n else (n, n + depth)
        extra[k, pl.ds(low * width, (high - low) * width), :] = residuals(
            left, low * width, (high - low) * width, lane_of, misfit[pl.ds(k, 1), :]
        )
        for p in range(k + 1, depth + 2 * REACH - 1 - k):
            for r, c, total in around(s, p, width, first, last):
                lap = total - 6.0 * c
                here = (p, pl.ds(GUARD + r, 8), slice(None))
                d[here] = 2.0 * c - d[here] + mod[p, pl.ds(r, 8), :] * lap
                if REACH <= p < REACH + depth:
                    lap_out[k, p - REACH, pl.ds(r, 8), :] = lap

        @pl.when((src_row >= (k + 1) * width) & (src_row < (depth + 2 * REACH - 1 - k) * width))
        def _():
            plane = src_row // width
            here = (plane, pl.ds(GUARD + src_row - plane * width, 1), slice(None))
            at = lax.broadcasted_iota(jnp.int32, (1, LANES), 1) == src_lane
            d[here] = d[here] + jnp.where(at, amplitude[0, k], 0.0)

    u, u_later = bufs[ITERS % 2], bufs[(ITERS + 1) % 2]
    rows = pl.ds(GUARD, width)
    even = is_even()
    a_edge[...] = u[jnp.where(even, REACH + depth - 1, REACH), rows, :]
    b_edge[...] = u[jnp.where(even, REACH, REACH + depth - 1), rows, :]
    for p in range(depth):
        u_out[p] = u[REACH + p, rows, :]
        later_out[p] = u_later[REACH + p, rows, :]


def adjoint_kernel(
    depth, width, shots, now, later, a_in, b_in, mod, weight, laps, extra, ua_edge, ub_edge,
    a_out, later_out, a_edge, b_edge, *rest
):
    *pieces, image, cur, old = rest
    n = REACH - 1
    clear_guards(cur)
    clear_guards(old)
    fill(
        depth, width, n, (now, later),
        ((a_in, 0, n), (a_in, n, n - 1)), ((b_in, 0, n), (b_in, n, n - 1)),
        (cur, old),
    )
    first, last = edges()
    bufs = (cur, old)

    def imaged(k, p, r, c):
        into = pl.ds((p - n) * width + r, 8)
        add = c * laps[k, p - n, pl.ds(r, 8), :]
        image[into, :] = image[into, :] + add if k > 0 else add

    for k in range(n):
        s, d = bufs[k % 2], bufs[(k + 1) % 2]
        for p in range(k + 1, depth + 2 * n - 1 - k):
            for r, c, total in around(s, p, width, first, last):
                here = (p, pl.ds(GUARD + r, 8), slice(None))
                rows = pl.ds(r, 8)
                new = weight[p + 1, rows, :] * c - d[here] + mod[p + 1, rows, :] * total
                d[here] = new + extra[k, pl.ds(p * width + r, 8), :]
                if n <= p < n + depth:
                    imaged(k, p, r, c)

    a, a_later = bufs[n % 2], bufs[(n + 1) % 2]
    for p in range(n, n + depth):
        for r in range(0, width, 8):
            imaged(n, p, r, a[p, pl.ds(GUARD + r, 8), :])
    size = depth * width // shots
    me = lax.axis_index("shot")
    for m in range(shots):
        to = me if m == 0 else send_slot(me, m, shots)
        pieces[m][...] = image[pl.ds(pl.multiple_of(to * size, size), size), :]
    rows = pl.ds(GUARD, width)
    for p in range(depth):
        a_out[p] = a[n + p, rows, :]
        later_out[p] = a_later[n + p, rows, :]
    even = is_even()
    a_edge[0] = ua_edge[...]
    b_edge[0] = ub_edge[...]
    a_edge[1] = a[jnp.where(even, n + depth - 1, n), rows, :]
    b_edge[1] = a[jnp.where(even, n, n + depth - 1), rows, :]


def last_kernel(
    depth, width, u, u_later, a, a_later, a_in, b_in, mod, weight, extra,
    base_out, lap_out, adjoint_out,
    upad, apad,
):
    n = REACH - 1
    clear_guards(upad)
    clear_guards(apad)
    fill(
        depth, width, 1, (u, a), ((a_in, 0, 1), (a_in, 1, 1)), ((b_in, 0, 1), (b_in, 1, 1)),
        (upad, apad),
    )
    first, last = edges()
    for p in range(depth):
        for r, c, total in around(upad, p + 1, width, first, last):
            rows = pl.ds(r, 8)
            lap_out[p, rows, :] = total - 6.0 * c
            base_out[p, rows, :] = 2.0 * c - u_later[p, rows, :]
        for r, c, total in around(apad, p + 1, width, first, last):
            rows = pl.ds(r, 8)
            q = REACH + p
            new = weight[q, rows, :] * c - a_later[p, rows, :] + mod[q, rows, :] * total
            adjoint_out[p, rows, :] = new + extra[n, pl.ds((n + p) * width + r, 8), :]


def sum_kernel(*refs):
    *parts, out = refs
    n = parts[0].shape[0]
    top = jnp.zeros((8, LANES), jnp.float32)
    for r in range(0, n, 8):
        total = parts[0][pl.ds(r, 8), :]
        for part in parts[1:]:
            total = total + part[pl.ds(r, 8), :]
        out[pl.ds(r, 8), :] = total
        top = jnp.maximum(top, jnp.abs(total))
    out[pl.ds(n, 8), :] = top


def top_kernel(*refs):
    *parts, out = refs
    n = parts[0].shape[0] - 8
    top = parts[0][pl.ds(n, 8), :]
    for part in parts[1:]:
        top = jnp.maximum(top, part[pl.ds(n, 8), :])
    out[...] = top


def update_kernel(depth, width, shots, *refs):
    grads, refs = refs[:shots], refs[shots:]
    *tops, model, base, laps, new_model, stepped, grad = refs
    n = depth * width // shots
    me = lax.axis_index("shot")
    for m in range(shots):
        owner = me if m == 0 else from_slot(me, m, shots)
        grad[pl.ds(pl.multiple_of(owner * n, n), n), :] = grads[m][pl.ds(0, n), :]
    top = tops[0][...]
    for other in tops[1:]:
        top = jnp.maximum(top, other[...])
    peak = jnp.max(top)
    for p in range(depth):
        for r in range(0, width, 8):
            g = grad[pl.ds(p * width + r, 8), :]
            rows = pl.ds(r, 8)
            new = jnp.clip(model[p, rows, :] - 0.1 * g / (peak + 1e-06), 0.05, 0.3)
            new_model[p, rows, :] = new
            stepped[p, rows, :] = base[p, rows, :] + new * laps[p, rows, :]


def placed(x, space):
    if space is VMEM or space is pltpu.HBM:
        return pltpu.with_memory_space_constraint(x, space)
    return x


def call(kernel, outs, args, spaces, scratch, flops, nbytes):
    args = [placed(x, space) for x, space in zip(args, spaces)]
    return pl.pallas_call(
        kernel,
        out_shape=outs,
        in_specs=[spec(space) for space in spaces],
        out_specs=[spec(VMEM)] * len(outs),
        scratch_shapes=scratch,
        cost_estimate=cost(flops, nbytes),
        compiler_params=pltpu.CompilerParams(vmem_limit_bytes=LIMIT),
    )(*args)


def per_device(model, fwd_now, fwd_next, adj_now, adj_next, wavelet, misfit, src_index, rec_index):
    f32 = jnp.float32
    depth, width, length = model.shape
    assert length == LANES and fwd_now.shape[0] == 1 and width % 8 == 0 and depth == REACH
    u0, u1, a0, a1 = fwd_now[0], fwd_next[0], adj_now[0], adj_next[0]
    slabs, shots = lax.axis_size("slab"), lax.axis_size("shot")
    perm_a, perm_b = pairs(slabs, 0), pairs(slabs, 1)
    planes = depth + 2 * REACH
    cells = depth * width * LANES
    own = VMEM((depth, width, LANES), f32)
    wide = VMEM((planes, width, LANES), f32)
    field = VMEM((planes, width + 2 * GUARD, LANES), f32)
    edge = VMEM((width, LANES), f32)
    out = jax.ShapeDtypeStruct((depth, width, LANES), f32)
    n = REACH - 1

    def exchange(to_a, to_b):
        b = lax.ppermute(to_b, "slab", perm_b)
        return lax.ppermute(to_a, "slab", perm_a), b

    def packed(args, sizes):
        total = sum(sizes)
        to_a, to_b, *whole = call(
            functools.partial(pack_kernel, depth, sizes),
            [VMEM((total, width, LANES), f32)] * 2 + [VMEM(x.shape, x.dtype) for x in args],
            args, [pltpu.HBM] * len(args),
            [pltpu.SemaphoreType.DMA((2, len(sizes))), pltpu.SemaphoreType.DMA((len(args),))],
            0, 4 * 4 * total * width * LANES,
        )
        return (to_a, to_b), whole

    ua, ub = exchange(u0, u0)
    to, (u1, model, u0) = packed((u1, model, u0), (n, n))
    ha, hb = exchange(*to)
    to, (a0, a1, rec_index, misfit) = packed((a0, a1, rec_index, misfit[0]), (n, n - 1))
    ga, gb = exchange(*to)
    near = depth + 2 * n
    u, u_later, laps, ua_edge, ub_edge, mod, weight, extra = call(
        functools.partial(forward_kernel, depth, width),
        [
            own, own, VMEM((ITERS, depth, width, LANES), f32), edge, edge, wide, wide,
            VMEM((ITERS, near * width, LANES), f32),
        ],
        (wavelet, src_index, rec_index, misfit, u0, u1, model, ua, ub, ha, hb),
        [pltpu.HBM, SMEM] + [VMEM] * 9,
        [
            SMEM(wavelet.shape, f32), pltpu.SemaphoreType.DMA,
            VMEM((near * width, 3 * LANES), jnp.bfloat16), field, field,
        ],
        15 * ITERS * 2 * cells, 80 * cells,
    )
    rows = depth * width // shots
    both = VMEM((2, width, LANES), f32)
    field = VMEM((near, width + 2 * GUARD, LANES), f32)
    a, a_later, a_edge, b_edge, *pieces = call(
        functools.partial(adjoint_kernel, depth, width, shots),
        [own, own, both, both] + [VMEM((rows, LANES), f32)] * shots,
        (a0, a1, ga, gb, mod, weight, laps, extra, ua_edge, ub_edge), [VMEM] * 10,
        [VMEM((depth * width, LANES), f32), field, field],
        18 * ITERS * 2 * cells, 80 * cells,
    )

    def with_others(own_one, pieces, axis):
        got, perms = {}, partner_perms(lax.axis_size(axis))
        for m in far_first(len(perms) + 1):
            got[m] = lax.ppermute(pieces[m], axis, perms[m])
        return [own_one] + [got[m] for m in sorted(got)]

    parts = with_others(pieces[0], pieces, "shot")
    a_edge, b_edge = exchange(a_edge, b_edge)
    (grad,) = call(
        sum_kernel, [VMEM((rows + 8, LANES), f32)], parts, [VMEM] * shots, [],
        shots * rows * LANES, 4 * shots * rows * LANES,
    )
    grads = with_others(grad, [grad] * shots, "shot")
    pad = VMEM((depth + 2, width + 2 * GUARD, LANES), f32)
    base, lap, a = call(
        functools.partial(last_kernel, depth, width), [own, own, out],
        (u, u_later, a, a_later, a_edge, b_edge, mod, weight, extra), [VMEM] * 9,
        [pad, pad], 30 * cells, 32 * cells,
    )
    (top,) = call(top_kernel, [VMEM((8, LANES), f32)], grads, [VMEM] * shots, [], 0, 4096 * shots)
    tops = with_others(top, [top] * slabs, "slab")
    new_model, stepped = call(
        functools.partial(update_kernel, depth, width, shots), [out, out],
        (*grads, *tops, model, base, lap), [VMEM] * (shots + slabs + 3),
        [VMEM((depth * width, LANES), f32)], 10 * cells, 4 * 6 * cells,
    )
    return new_model, stepped[None], a[None]


def solution(mesh):
    in_specs = (
        P(("groups", "slab"), None, None),
        P(("groups", "shot"), "slab", None, None),
        P(("groups", "shot"), "slab", None, None),
        P(("groups", "shot"), "slab", None, None),
        P(("groups", "shot"), "slab", None, None),
        P(("groups", "shot"), None),
        P(("groups", "shot"), None, None),
        P(("groups", "shot")),
        P(("groups", "shot"), None),
    )
    out_specs = (
        P(("groups", "slab"), None, None),
        P(("groups", "shot"), "slab", None, None),
        P(("groups", "shot"), "slab", None, None),
    )
    return jax.shard_map(per_device, mesh=mesh, in_specs=in_specs, out_specs=out_specs, check_vma=False)
```

```python
import functools

import jax
import jax.numpy as jnp
from jax import lax
from jax.experimental import pallas as pl
from jax.experimental.pallas import tpu as pltpu
from jax.sharding import PartitionSpec as P

ITERS = 8
REACH = ITERS
GUARD = 8
LANES = 128
LIMIT = 16 * 2**20
VMEM = pltpu.VMEM
SMEM = pltpu.SMEM


def pairs(count, start):
    low = [(i, i + 1) for i in range(start, count - 1, 2)]
    return low + [(b, a) for a, b in low]


def partner_perms(count):
    if count & (count - 1) == 0:
        return {m: [(i, i ^ m) for i in range(count)] for m in range(1, count)}
    return {m: [(i, (i + m) % count) for i in range(count)] for m in range(1, count)}


def far_first(count):
    half = count // 2
    return [*range(half, count), *range(1, half)]


def send_slot(me, m, count):
    return me ^ m if count & (count - 1) == 0 else lax.rem(me + m, count)


def from_slot(me, m, count):
    return me ^ m if count & (count - 1) == 0 else lax.rem(me - m + count, count)


def spec(space):
    return pl.BlockSpec(memory_space=space)


def cost(flops, nbytes):
    return pl.CostEstimate(flops=int(flops), bytes_accessed=int(nbytes), transcendentals=0)


def is_even():
    return lax.rem(lax.axis_index("slab"), 2) == 0


def pack_kernel(depth, sizes, *refs):
    count = (len(refs) - 4) // 2
    args, (to_a, to_b), whole, (sem, own_sem) = (
        refs[:count], refs[count : count + 2], refs[count + 2 : -2], refs[-2:],
    )

    def copies(up_a, up_b):
        out = []
        for j, (dst, up) in enumerate(((to_a, up_a), (to_b, up_b))):
            at = 0
            for i, (field, size) in enumerate(zip(args, sizes)):
                out.append(
                    pltpu.make_async_copy(
                        field.at[pl.ds(depth - size if up else 0, size)],
                        dst.at[pl.ds(at, size)],
                        sem.at[j, i],
                    )
                )
                at += size
        return out

    even = is_even()

    @pl.when(even)
    def _():
        for c in copies(True, False):
            c.start()

    @pl.when(jnp.logical_not(even))
    def _():
        for c in copies(False, True):
            c.start()

    own = [
        pltpu.make_async_copy(src, dst, own_sem.at[i]) for i, (src, dst) in enumerate(zip(args, whole))
    ]
    for c in own:
        c.start()
    for c in copies(False, False) + own:
        c.wait()


def hot_rows(base, rec_ref, left):
    index = rec_ref[...]
    row_of = index // LANES
    lane_of = index - row_of * LANES
    row_of = row_of - base
    group = 128
    for first in range(0, left.shape[0], group):
        at = lax.broadcasted_iota(jnp.int32, (group, LANES), 0) + first
        hot = jnp.where(at == row_of, 1.0, 0.0).astype(jnp.bfloat16)
        for part in range(3):
            left[pl.ds(first, group), pl.ds(part * LANES, LANES)] = hot
    return lane_of


def residuals(left, first, size, lane_of, value):
    mine = lax.broadcasted_iota(jnp.int32, (LANES, LANES), 0) == lane_of
    parts = []
    for _ in range(3):
        piece = value.astype(jnp.bfloat16).astype(jnp.float32)
        value = value - piece
        parts.append(jnp.where(mine, piece, 0.0).astype(jnp.bfloat16))
    return lax.dot_general(
        left[pl.ds(first, size), :], jnp.concatenate(parts, axis=1),
        (((1,), (1,)), ((), ())), preferred_element_type=jnp.float32,
    )


def around(src, p, width, first, last):
    starts = range(GUARD, GUARD + width, 8)
    here = [src[p, pl.ds(r, 8), :] for r in starts]
    after = [pltpu.roll(c, LANES - 1, 1) for c in here]
    before = [pltpu.roll(c, 1, 1) for c in here]
    out = []
    for r, c, x, y in zip(starts, here, after, before):
        s = src[p + 1, pl.ds(r, 8), :] + src[p - 1, pl.ds(r, 8), :]
        s = s + src[p, pl.ds(r + 1, 8), :]
        s = s + src[p, pl.ds(r - 1, 8), :]
        s = s + jnp.where(last, 0.0, x)
        s = s + jnp.where(first, 0.0, y)
        out.append((r - GUARD, c, s))
    return out


def edges():
    lane = lax.broadcasted_iota(jnp.int32, (8, LANES), 1)
    return lane == 0, lane == LANES - 1


def clear_guards(field):
    planes, rows, _ = field.shape
    zero = jnp.zeros((GUARD, LANES), jnp.float32)
    for p in range(planes):
        field[p, pl.ds(0, GUARD), :] = zero
        field[p, pl.ds(rows - GUARD, GUARD), :] = zero


def fill(depth, width, reach, own, a_in, b_in, bufs):
    rows = [pl.ds(GUARD if buf.shape[1] > width else 0, width) for buf in bufs]
    for src, buf, r in zip(own, bufs, rows):
        for p in range(depth):
            buf[reach + p, r, :] = src[p]

    def put(low, high):
        for buf, r, (lo, at, size), (hi, _, _) in zip(bufs, rows, low, high):
            for p in range(size):
                buf[reach - size + p, r, :] = lo[at + p]
                buf[reach + depth + p, r, :] = hi[at + p]

    even = is_even()

    @pl.when(even)
    def _():
        put(b_in, a_in)

    @pl.when(jnp.logical_not(even))
    def _():
        put(a_in, b_in)


def forward_kernel(
    depth, width, wavelet, src_index, rec_index, misfit, now, later, model, ua_in, ub_in, ha_in, hb_in,
    u_out, later_out, lap_out, a_edge, b_edge, mod, weight, extra,
    amplitude, sem, left, cur, old,
):
    n = REACH - 1
    slab = lax.axis_index("slab")
    fetch = pltpu.make_async_copy(wavelet, amplitude, sem)
    fetch.start()
    clear_guards(cur)
    clear_guards(old)
    fill(
        depth, width, REACH, (now, later, model),
        ((ua_in, 0, REACH), (ha_in, 0, n), (ha_in, n, n)),
        ((ub_in, 0, REACH), (hb_in, 0, n), (hb_in, n, n)),
        (cur, old, mod),
    )
    lane_of = hot_rows((slab * depth - n) * width, rec_index, left)
    fetch.wait()
    for p in range(1, depth + 2 * REACH - 1):
        weight[p] = 2.0 - 6.0 * mod[p]
    first, last = edges()
    source = src_index[0]
    src_row = source // LANES
    src_lane = source - src_row * LANES
    src_row = src_row - (slab * depth - REACH) * width
    bufs = (cur, old)
    for k in range(ITERS):
        s, d = bufs[k % 2], bufs[(k + 1) % 2]
        low, high = (k + 1, depth + 2 * n - 1 - k) if k < n else (n, n + depth)
        extra[k, pl.ds(low * width, (high - low) * width), :] = residuals(
            left, low * width, (high - low) * width, lane_of, misfit[pl.ds(k, 1), :]
        )
        for p in range(k + 1, depth + 2 * REACH - 1 - k):
            for r, c, total in around(s, p, width, first, last):
                lap = total - 6.0 * c
                here = (p, pl.ds(GUARD + r, 8), slice(None))
                d[here] = 2.0 * c - d[here] + mod[p, pl.ds(r, 8), :] * lap
                if REACH <= p < REACH + depth:
                    lap_out[k, p - REACH, pl.ds(r, 8), :] = lap

        @pl.when((src_row >= (k + 1) * width) & (src_row < (depth + 2 * REACH - 1 - k) * width))
        def _():
            plane = src_row // width
            here = (plane, pl.ds(GUARD + src_row - plane * width, 1), slice(None))
            at = lax.broadcasted_iota(jnp.int32, (1, LANES), 1) == src_lane
            d[here] = d[here] + jnp.where(at, amplitude[0, k], 0.0)

    u, u_later = bufs[ITERS % 2], bufs[(ITERS + 1) % 2]
    rows = pl.ds(GUARD, width)
    even = is_even()
    a_edge[...] = u[jnp.where(even, REACH + depth - 1, REACH), rows, :]
    b_edge[...] = u[jnp.where(even, REACH, REACH + depth - 1), rows, :]
    for p in range(depth):
        u_out[p] = u[REACH + p, rows, :]
        later_out[p] = u_later[REACH + p, rows, :]


def adjoint_kernel(
    depth, width, shots, now, later, a_in, b_in, mod, weight, laps, extra, ua_edge, ub_edge,
    a_out, later_out, a_edge, b_edge, *rest
):
    *pieces, image, cur, old = rest
    n = REACH - 1
    clear_guards(cur)
    clear_guards(old)
    fill(
        depth, width, n, (now, later),
        ((a_in, 0, n), (a_in, n, n - 1)), ((b_in, 0, n), (b_in, n, n - 1)),
        (cur, old),
    )
    first, last = edges()
    bufs = (cur, old)

    def imaged(k, p, r, c):
        into = pl.ds((p - n) * width + r, 8)
        add = c * laps[k, p - n, pl.ds(r, 8), :]
        image[into, :] = image[into, :] + add if k > 0 else add

    for k in range(n):
        s, d = bufs[k % 2], bufs[(k + 1) % 2]
        for p in range(k + 1, depth + 2 * n - 1 - k):
            for r, c, total in around(s, p, width, first, last):
                here = (p, pl.ds(GUARD + r, 8), slice(None))
                rows = pl.ds(r, 8)
                new = weight[p + 1, rows, :] * c - d[here] + mod[p + 1, rows, :] * total
                d[here] = new + extra[k, pl.ds(p * width + r, 8), :]
                if n <= p < n + depth:
                    imaged(k, p, r, c)

    a, a_later = bufs[n % 2], bufs[(n + 1) % 2]
    for p in range(n, n + depth):
        for r in range(0, width, 8):
            imaged(n, p, r, a[p, pl.ds(GUARD + r, 8), :])
    size = depth * width // shots
    me = lax.axis_index("shot")
    for m in range(shots):
        to = me if m == 0 else send_slot(me, m, shots)
        pieces[m][...] = image[pl.ds(pl.multiple_of(to * size, size), size), :]
    rows = pl.ds(GUARD, width)
    for p in range(depth):
        a_out[p] = a[n + p, rows, :]
        later_out[p] = a_later[n + p, rows, :]
    even = is_even()
    a_edge[0] = ua_edge[...]
    b_edge[0] = ub_edge[...]
    a_edge[1] = a[jnp.where(even, n + depth - 1, n), rows, :]
    b_edge[1] = a[jnp.where(even, n, n + depth - 1), rows, :]


def last_kernel(
    depth, width, u, u_later, a, a_later, a_in, b_in, mod, weight, extra,
    base_out, lap_out, adjoint_out,
    upad, apad,
):
    n = REACH - 1
    clear_guards(upad)
    clear_guards(apad)
    fill(
        depth, width, 1, (u, a), ((a_in, 0, 1), (a_in, 1, 1)), ((b_in, 0, 1), (b_in, 1, 1)),
        (upad, apad),
    )
    first, last = edges()
    for p in range(depth):
        for r, c, total in around(upad, p + 1, width, first, last):
            rows = pl.ds(r, 8)
            lap_out[p, rows, :] = total - 6.0 * c
            base_out[p, rows, :] = 2.0 * c - u_later[p, rows, :]
        for r, c, total in around(apad, p + 1, width, first, last):
            rows = pl.ds(r, 8)
            q = REACH + p
            new = weight[q, rows, :] * c - a_later[p, rows, :] + mod[q, rows, :] * total
            adjoint_out[p, rows, :] = new + extra[n, pl.ds((n + p) * width + r, 8), :]


def sum_kernel(*refs):
    *parts, out, top_out = refs
    top = jnp.zeros((8, LANES), jnp.float32)
    for r in range(0, out.shape[0], 8):
        total = parts[0][pl.ds(r, 8), :]
        for part in parts[1:]:
            total = total + part[pl.ds(r, 8), :]
        out[pl.ds(r, 8), :] = total
        top = jnp.maximum(top, jnp.abs(total))
    top_out[...] = top


def top_kernel(grad, *refs):
    *parts, out = refs
    n = grad.shape[0]
    out[pl.ds(0, n), :] = grad[...]
    top = parts[0][...]
    for part in parts[1:]:
        top = jnp.maximum(top, part[...])
    out[pl.ds(n, 8), :] = top


def update_kernel(depth, width, shots, *refs):
    grads, refs = refs[:shots], refs[shots:]
    model, base, laps, new_model, stepped, grad = refs
    n = depth * width // shots
    me = lax.axis_index("shot")
    for m in range(shots):
        owner = me if m == 0 else from_slot(me, m, shots)
        grad[pl.ds(pl.multiple_of(owner * n, n), n), :] = grads[m][pl.ds(0, n), :]
    top = grads[0][pl.ds(n, 8), :]
    for other in grads[1:]:
        top = jnp.maximum(top, other[pl.ds(n, 8), :])
    peak = jnp.max(top)
    for p in range(depth):
        for r in range(0, width, 8):
            g = grad[pl.ds(p * width + r, 8), :]
            rows = pl.ds(r, 8)
            new = jnp.clip(model[p, rows, :] - 0.1 * g / (peak + 1e-06), 0.05, 0.3)
            new_model[p, rows, :] = new
            stepped[p, rows, :] = base[p, rows, :] + new * laps[p, rows, :]


def placed(x, space):
    if space is VMEM or space is pltpu.HBM:
        return pltpu.with_memory_space_constraint(x, space)
    return x


def call(kernel, outs, args, spaces, scratch, flops, nbytes):
    args = [placed(x, space) for x, space in zip(args, spaces)]
    return pl.pallas_call(
        kernel,
        out_shape=outs,
        in_specs=[spec(space) for space in spaces],
        out_specs=[spec(VMEM)] * len(outs),
        scratch_shapes=scratch,
        cost_estimate=cost(flops, nbytes),
        compiler_params=pltpu.CompilerParams(vmem_limit_bytes=LIMIT),
    )(*args)


def per_device(model, fwd_now, fwd_next, adj_now, adj_next, wavelet, misfit, src_index, rec_index):
    f32 = jnp.float32
    depth, width, length = model.shape
    assert length == LANES and fwd_now.shape[0] == 1 and width % 8 == 0 and depth == REACH
    u0, u1, a0, a1 = fwd_now[0], fwd_next[0], adj_now[0], adj_next[0]
    slabs, shots = lax.axis_size("slab"), lax.axis_size("shot")
    perm_a, perm_b = pairs(slabs, 0), pairs(slabs, 1)
    planes = depth + 2 * REACH
    cells = depth * width * LANES
    own = VMEM((depth, width, LANES), f32)
    wide = VMEM((planes, width, LANES), f32)
    field = VMEM((planes, width + 2 * GUARD, LANES), f32)
    edge = VMEM((width, LANES), f32)
    out = jax.ShapeDtypeStruct((depth, width, LANES), f32)
    n = REACH - 1

    def exchange(to_a, to_b):
        b = lax.ppermute(to_b, "slab", perm_b)
        return lax.ppermute(to_a, "slab", perm_a), b

    def packed(args, sizes):
        total = sum(sizes)
        to_a, to_b, *whole = call(
            functools.partial(pack_kernel, depth, sizes),
            [VMEM((total, width, LANES), f32)] * 2 + [VMEM(x.shape, x.dtype) for x in args],
            args, [pltpu.HBM] * len(args),
            [pltpu.SemaphoreType.DMA((2, len(sizes))), pltpu.SemaphoreType.DMA((len(args),))],
            0, 4 * 4 * total * width * LANES,
        )
        return (to_a, to_b), whole

    ua, ub = exchange(u0, u0)
    to, (u1, model, u0) = packed((u1, model, u0), (n, n))
    ha, hb = exchange(*to)
    to, (a0, a1, rec_index, misfit) = packed((a0, a1, rec_index, misfit[0]), (n, n - 1))
    ga, gb = exchange(*to)
    near = depth + 2 * n
    u, u_later, laps, ua_edge, ub_edge, mod, weight, extra = call(
        functools.partial(forward_kernel, depth, width),
        [
            own, own, VMEM((ITERS, depth, width, LANES), f32), edge, edge, wide, wide,
            VMEM((ITERS, near * width, LANES), f32),
        ],
        (wavelet, src_index, rec_index, misfit, u0, u1, model, ua, ub, ha, hb),
        [pltpu.HBM, SMEM] + [VMEM] * 9,
        [
            SMEM(wavelet.shape, f32), pltpu.SemaphoreType.DMA,
            VMEM((near * width, 3 * LANES), jnp.bfloat16), field, field,
        ],
        15 * ITERS * 2 * cells, 80 * cells,
    )
    rows = depth * width // shots
    both = VMEM((2, width, LANES), f32)
    field = VMEM((near, width + 2 * GUARD, LANES), f32)
    a, a_later, a_edge, b_edge, *pieces = call(
        functools.partial(adjoint_kernel, depth, width, shots),
        [own, own, both, both] + [VMEM((rows, LANES), f32)] * shots,
        (a0, a1, ga, gb, mod, weight, laps, extra, ua_edge, ub_edge), [VMEM] * 10,
        [VMEM((depth * width, LANES), f32), field, field],
        18 * ITERS * 2 * cells, 80 * cells,
    )

    def with_others(own_one, pieces, axis):
        got, perms = {}, partner_perms(lax.axis_size(axis))
        for m in far_first(len(perms) + 1):
            got[m] = lax.ppermute(pieces[m], axis, perms[m])
        return [own_one] + [got[m] for m in sorted(got)]

    parts = with_others(pieces[0], pieces, "shot")
    a_edge, b_edge = exchange(a_edge, b_edge)
    tile = VMEM((8, LANES), f32)
    grad, top = call(
        sum_kernel, [VMEM((rows, LANES), f32), tile], parts, [VMEM] * shots, [],
        shots * rows * LANES, 4 * shots * rows * LANES,
    )
    tops = with_others(top, [top] * slabs, "slab")
    (grad,) = call(
        top_kernel, [VMEM((rows + 8, LANES), f32)], [grad, *tops], [VMEM] * (slabs + 1), [],
        0, 4096 * shots,
    )
    grads = with_others(grad, [grad] * shots, "shot")
    pad = VMEM((depth + 2, width + 2 * GUARD, LANES), f32)
    base, lap, a = call(
        functools.partial(last_kernel, depth, width), [own, own, out],
        (u, u_later, a, a_later, a_edge, b_edge, mod, weight, extra), [VMEM] * 9,
        [pad, pad], 30 * cells, 32 * cells,
    )
    new_model, stepped = call(
        functools.partial(update_kernel, depth, width, shots), [out, out],
        (*grads, model, base, lap), [VMEM] * (shots + 3),
        [VMEM((depth * width, LANES), f32)], 10 * cells, 4 * 6 * cells,
    )
    return new_model, stepped[None], a[None]


def solution(mesh):
    in_specs = (
        P(("groups", "slab"), None, None),
        P(("groups", "shot"), "slab", None, None),
        P(("groups", "shot"), "slab", None, None),
        P(("groups", "shot"), "slab", None, None),
        P(("groups", "shot"), "slab", None, None),
        P(("groups", "shot"), None),
        P(("groups", "shot"), None, None),
        P(("groups", "shot")),
        P(("groups", "shot"), None),
    )
    out_specs = (
        P(("groups", "slab"), None, None),
        P(("groups", "shot"), "slab", None, None),
        P(("groups", "shot"), "slab", None, None),
    )
    return jax.shard_map(per_device, mesh=mesh, in_specs=in_specs, out_specs=out_specs, check_vma=False)
```

```python
import functools

import jax
import jax.numpy as jnp
from jax import lax
from jax.experimental import pallas as pl
from jax.experimental.pallas import tpu as pltpu
from jax.sharding import PartitionSpec as P


ITERS = 8
REACH = ITERS
GUARD = 8
LANES = 128
LIMIT = 16 * 2**20
VMEM = pltpu.VMEM
SMEM = pltpu.SMEM


def pairs(count, start):
    low = [(i, i + 1) for i in range(start, count - 1, 2)]
    return low + [(b, a) for a, b in low]


def partner_perms(count):
    if count & (count - 1) == 0:
        return {m: [(i, i ^ m) for i in range(count)] for m in range(1, count)}
    return {m: [(i, (i + m) % count) for i in range(count)] for m in range(1, count)}


def far_first(count):
    half = count // 2
    return [*range(half, count), *range(1, half)]


def send_slot(me, m, count):
    return me ^ m if count & (count - 1) == 0 else lax.rem(me + m, count)


def from_slot(me, m, count):
    return me ^ m if count & (count - 1) == 0 else lax.rem(me - m + count, count)


def spec(space):
    return pl.BlockSpec(memory_space=space)


def cost(flops, nbytes):
    return pl.CostEstimate(flops=int(flops), bytes_accessed=int(nbytes), transcendentals=0)


def is_even():
    return lax.rem(lax.axis_index("slab"), 2) == 0


def pack_kernel(depth, sizes, *refs):
    count = (len(refs) - 4) // 2
    args, (to_a, to_b), whole, (sem, own_sem) = (
        refs[:count], refs[count : count + 2], refs[count + 2 : -2], refs[-2:],
    )

    def copies(up_a, up_b):
        out = []
        for j, (dst, up) in enumerate(((to_a, up_a), (to_b, up_b))):
            at = 0
            for i, (field, size) in enumerate(zip(args, sizes)):
                out.append(
                    pltpu.make_async_copy(
                        field.at[pl.ds(depth - size if up else 0, size)],
                        dst.at[pl.ds(at, size)],
                        sem.at[j, i],
                    )
                )
                at += size
        return out

    even = is_even()

    @pl.when(even)
    def _():
        for c in copies(True, False):
            c.start()

    @pl.when(jnp.logical_not(even))
    def _():
        for c in copies(False, True):
            c.start()

    own = [
        pltpu.make_async_copy(src, dst, own_sem.at[i]) for i, (src, dst) in enumerate(zip(args, whole))
    ]
    for c in own:
        c.start()
    for c in copies(False, False) + own:
        c.wait()


def hot_rows(base, rec_ref, left):
    index = rec_ref[...]
    row_of = index // LANES
    lane_of = index - row_of * LANES
    row_of = row_of - base
    group = 128
    for first in range(0, left.shape[0], group):
        at = lax.broadcasted_iota(jnp.int32, (group, LANES), 0) + first
        hot = jnp.where(at == row_of, 1.0, 0.0).astype(jnp.bfloat16)
        for part in range(3):
            left[pl.ds(first, group), pl.ds(part * LANES, LANES)] = hot
    return lane_of


def residuals(left, first, size, lane_of, value):
    mine = lax.broadcasted_iota(jnp.int32, (LANES, LANES), 0) == lane_of
    parts = []
    for _ in range(3):
        piece = value.astype(jnp.bfloat16).astype(jnp.float32)
        value = value - piece
        parts.append(jnp.where(mine, piece, 0.0).astype(jnp.bfloat16))
    return lax.dot_general(
        left[pl.ds(first, size), :], jnp.concatenate(parts, axis=1),
        (((1,), (1,)), ((), ())), preferred_element_type=jnp.float32,
    )


def around(src, p, width, first, last):
    starts = range(GUARD, GUARD + width, 8)
    here = [src[p, pl.ds(r, 8), :] for r in starts]
    after = [pltpu.roll(c, LANES - 1, 1) for c in here]
    before = [pltpu.roll(c, 1, 1) for c in here]
    out = []
    for r, c, x, y in zip(starts, here, after, before):
        s = src[p + 1, pl.ds(r, 8), :] + src[p - 1, pl.ds(r, 8), :]
        s = s + src[p, pl.ds(r + 1, 8), :]
        s = s + src[p, pl.ds(r - 1, 8), :]
        s = s + jnp.where(last, 0.0, x)
        s = s + jnp.where(first, 0.0, y)
        out.append((r - GUARD, c, s))
    return out


def edges():
    lane = lax.broadcasted_iota(jnp.int32, (8, LANES), 1)
    return lane == 0, lane == LANES - 1


def clear_guards(field):
    planes, rows, _ = field.shape
    zero = jnp.zeros((GUARD, LANES), jnp.float32)
    for p in range(planes):
        field[p, pl.ds(0, GUARD), :] = zero
        field[p, pl.ds(rows - GUARD, GUARD), :] = zero


def fill(depth, width, reach, own, a_in, b_in, bufs):
    rows = [pl.ds(GUARD if buf.shape[1] > width else 0, width) for buf in bufs]
    for src, buf, r in zip(own, bufs, rows):
        for p in range(depth):
            buf[reach + p, r, :] = src[p]

    def put(low, high):
        for buf, r, (lo, at, size), (hi, _, _) in zip(bufs, rows, low, high):
            for p in range(size):
                buf[reach - size + p, r, :] = lo[at + p]
                buf[reach + depth + p, r, :] = hi[at + p]

    even = is_even()

    @pl.when(even)
    def _():
        put(b_in, a_in)

    @pl.when(jnp.logical_not(even))
    def _():
        put(a_in, b_in)


def forward_kernel(
    depth, width, wavelet, src_index, rec_index, misfit, now, later, model, ua_in, ub_in, ha_in, hb_in,
    u_out, later_out, lap_out, a_edge, b_edge, mod, weight, extra,
    amplitude, sem, left, cur, old,
):
    n = REACH - 1
    slab = lax.axis_index("slab")
    fetch = pltpu.make_async_copy(wavelet, amplitude, sem)
    fetch.start()
    clear_guards(cur)
    clear_guards(old)
    fill(
        depth, width, REACH, (now, later, model),
        ((ua_in, 0, REACH), (ha_in, 0, n), (ha_in, n, n)),
        ((ub_in, 0, REACH), (hb_in, 0, n), (hb_in, n, n)),
        (cur, old, mod),
    )
    lane_of = hot_rows((slab * depth - n) * width, rec_index, left)
    fetch.wait()
    for p in range(1, depth + 2 * REACH - 1):
        weight[p] = 2.0 - 6.0 * mod[p]
    first, last = edges()
    source = src_index[0]
    src_row = source // LANES
    src_lane = source - src_row * LANES
    src_row = src_row - (slab * depth - REACH) * width
    bufs = (cur, old)
    for k in range(ITERS):
        s, d = bufs[k % 2], bufs[(k + 1) % 2]
        low, high = (k + 1, depth + 2 * n - 1 - k) if k < n else (n, n + depth)
        extra[k, pl.ds(low * width, (high - low) * width), :] = residuals(
            left, low * width, (high - low) * width, lane_of, misfit[pl.ds(k, 1), :]
        )
        for p in range(k + 1, depth + 2 * REACH - 1 - k):
            for r, c, total in around(s, p, width, first, last):
                lap = total - 6.0 * c
                here = (p, pl.ds(GUARD + r, 8), slice(None))
                d[here] = 2.0 * c - d[here] + mod[p, pl.ds(r, 8), :] * lap
                if REACH <= p < REACH + depth:
                    lap_out[k, p - REACH, pl.ds(r, 8), :] = lap

        @pl.when((src_row >= (k + 1) * width) & (src_row < (depth + 2 * REACH - 1 - k) * width))
        def _():
            plane = src_row // width
            here = (plane, pl.ds(GUARD + src_row - plane * width, 1), slice(None))
            at = lax.broadcasted_iota(jnp.int32, (1, LANES), 1) == src_lane
            d[here] = d[here] + jnp.where(at, amplitude[0, k], 0.0)

    u, u_later = bufs[ITERS % 2], bufs[(ITERS + 1) % 2]
    rows = pl.ds(GUARD, width)
    even = is_even()
    a_edge[...] = u[jnp.where(even, REACH + depth - 1, REACH), rows, :]
    b_edge[...] = u[jnp.where(even, REACH, REACH + depth - 1), rows, :]
    for p in range(depth):
        u_out[p] = u[REACH + p, rows, :]
        later_out[p] = u_later[REACH + p, rows, :]


def adjoint_kernel(
    depth, width, shots, now, later, a_in, b_in, mod, weight, laps, extra, ua_edge, ub_edge,
    a_out, later_out, a_edge, b_edge, *rest
):
    *pieces, image, cur, old = rest
    n = REACH - 1
    clear_guards(cur)
    clear_guards(old)
    fill(
        depth, width, n, (now, later),
        ((a_in, 0, n), (a_in, n, n - 1)), ((b_in, 0, n), (b_in, n, n - 1)),
        (cur, old),
    )
    first, last = edges()
    bufs = (cur, old)

    def imaged(k, p, r, c):
        into = pl.ds((p - n) * width + r, 8)
        add = c * laps[k, p - n, pl.ds(r, 8), :]
        image[into, :] = image[into, :] + add if k > 0 else add

    for k in range(n):
        s, d = bufs[k % 2], bufs[(k + 1) % 2]
        for p in range(k + 1, depth + 2 * n - 1 - k):
            for r, c, total in around(s, p, width, first, last):
                here = (p, pl.ds(GUARD + r, 8), slice(None))
                rows = pl.ds(r, 8)
                new = weight[p + 1, rows, :] * c - d[here] + mod[p + 1, rows, :] * total
                d[here] = new + extra[k, pl.ds(p * width + r, 8), :]
                if n <= p < n + depth:
                    imaged(k, p, r, c)

    a, a_later = bufs[n % 2], bufs[(n + 1) % 2]
    for p in range(n, n + depth):
        for r in range(0, width, 8):
            imaged(n, p, r, a[p, pl.ds(GUARD + r, 8), :])
    size = depth * width // shots
    me = lax.axis_index("shot")
    for m in range(shots):
        to = me if m == 0 else send_slot(me, m, shots)
        pieces[m][...] = image[pl.ds(pl.multiple_of(to * size, size), size), :]
    rows = pl.ds(GUARD, width)
    for p in range(depth):
        a_out[p] = a[n + p, rows, :]
        later_out[p] = a_later[n + p, rows, :]
    even = is_even()
    a_edge[0] = ua_edge[...]
    b_edge[0] = ub_edge[...]
    a_edge[1] = a[jnp.where(even, n + depth - 1, n), rows, :]
    b_edge[1] = a[jnp.where(even, n, n + depth - 1), rows, :]


def last_kernel(
    depth, width, u, u_later, a, a_later, a_in, b_in, mod, weight, extra,
    base_out, lap_out, adjoint_out,
    upad, apad,
):
    n = REACH - 1
    clear_guards(upad)
    clear_guards(apad)
    fill(
        depth, width, 1, (u, a), ((a_in, 0, 1), (a_in, 1, 1)), ((b_in, 0, 1), (b_in, 1, 1)),
        (upad, apad),
    )
    first, last = edges()
    for p in range(depth):
        for r, c, total in around(upad, p + 1, width, first, last):
            rows = pl.ds(r, 8)
            lap_out[p, rows, :] = total - 6.0 * c
            base_out[p, rows, :] = 2.0 * c - u_later[p, rows, :]
        for r, c, total in around(apad, p + 1, width, first, last):
            rows = pl.ds(r, 8)
            q = REACH + p
            new = weight[q, rows, :] * c - a_later[p, rows, :] + mod[q, rows, :] * total
            adjoint_out[p, rows, :] = new + extra[n, pl.ds((n + p) * width + r, 8), :]


def sum_kernel(*refs):
    *parts, out, top_out = refs
    top = jnp.zeros((8, LANES), jnp.float32)
    for r in range(0, out.shape[0], 8):
        total = parts[0][pl.ds(r, 8), :]
        for part in parts[1:]:
            total = total + part[pl.ds(r, 8), :]
        out[pl.ds(r, 8), :] = total
        top = jnp.maximum(top, jnp.abs(total))
    top_out[...] = top


def top_kernel(grad, *refs):
    *parts, out = refs
    n = grad.shape[0]
    out[pl.ds(0, n), :] = grad[...]
    top = parts[0][...]
    for part in parts[1:]:
        top = jnp.maximum(top, part[...])
    out[pl.ds(n, 8), :] = top


def update_kernel(depth, width, shots, *refs):
    grads, refs = refs[:shots], refs[shots:]
    model, base, laps, new_model, stepped, grad = refs
    n = depth * width // shots
    me = lax.axis_index("shot")
    for m in range(shots):
        owner = me if m == 0 else from_slot(me, m, shots)
        grad[pl.ds(pl.multiple_of(owner * n, n), n), :] = grads[m][pl.ds(0, n), :]
    top = grads[0][pl.ds(n, 8), :]
    for other in grads[1:]:
        top = jnp.maximum(top, other[pl.ds(n, 8), :])
    peak = jnp.max(top)
    for p in range(depth):
        for r in range(0, width, 8):
            g = grad[pl.ds(p * width + r, 8), :]
            rows = pl.ds(r, 8)
            new = jnp.clip(model[p, rows, :] - 0.1 * g / (peak + 1e-06), 0.05, 0.3)
            new_model[p, rows, :] = new
            stepped[p, rows, :] = base[p, rows, :] + new * laps[p, rows, :]


def placed(x, space):
    if space is VMEM or space is pltpu.HBM:
        return pltpu.with_memory_space_constraint(x, space)
    return x


def call(kernel, outs, args, spaces, scratch, flops, nbytes):
    args = [placed(x, space) for x, space in zip(args, spaces)]
    return pl.pallas_call(
        kernel,
        out_shape=outs,
        in_specs=[spec(space) for space in spaces],
        out_specs=[spec(VMEM)] * len(outs),
        scratch_shapes=scratch,
        cost_estimate=cost(flops, nbytes),
        compiler_params=pltpu.CompilerParams(vmem_limit_bytes=LIMIT),
    )(*args)


def per_device(model, fwd_now, fwd_next, adj_now, adj_next, wavelet, misfit, src_index, rec_index):
    f32 = jnp.float32
    depth, width, length = model.shape
    assert length == LANES and fwd_now.shape[0] == 1 and width % 8 == 0 and depth == REACH
    u0, u1, a0, a1 = fwd_now[0], fwd_next[0], adj_now[0], adj_next[0]
    slabs, shots = lax.axis_size("slab"), lax.axis_size("shot")
    perm_a, perm_b = pairs(slabs, 0), pairs(slabs, 1)
    planes = depth + 2 * REACH
    cells = depth * width * LANES
    own = VMEM((depth, width, LANES), f32)
    wide = VMEM((planes, width, LANES), f32)
    field = VMEM((planes, width + 2 * GUARD, LANES), f32)
    edge = VMEM((width, LANES), f32)
    out = jax.ShapeDtypeStruct((depth, width, LANES), f32)
    n = REACH - 1

    def exchange(to_a, to_b):
        b = lax.ppermute(to_b, "slab", perm_b)
        return lax.ppermute(to_a, "slab", perm_a), b

    def packed(args, sizes):
        total = sum(sizes)
        to_a, to_b, *whole = call(
            functools.partial(pack_kernel, depth, sizes),
            [VMEM((total, width, LANES), f32)] * 2 + [VMEM(x.shape, x.dtype) for x in args],
            args, [pltpu.HBM] * len(args),
            [pltpu.SemaphoreType.DMA((2, len(sizes))), pltpu.SemaphoreType.DMA((len(args),))],
            0, 4 * 4 * total * width * LANES,
        )
        return (to_a, to_b), whole

    ua, ub = exchange(u0, u0)
    to, (u1, model, u0) = packed((u1, model, u0), (n, n))
    ha, hb = exchange(*to)
    to, (a0, a1, rec_index, misfit) = packed((a0, a1, rec_index, misfit[0]), (n, n - 1))
    ga, gb = exchange(*to)
    near = depth + 2 * n
    u, u_later, laps, ua_edge, ub_edge, mod, weight, extra = call(
        functools.partial(forward_kernel, depth, width),
        [
            own, own, VMEM((ITERS, depth, width, LANES), f32), edge, edge, wide, wide,
            VMEM((ITERS, near * width, LANES), f32),
        ],
        (wavelet, src_index, rec_index, misfit, u0, u1, model, ua, ub, ha, hb),
        [pltpu.HBM, SMEM] + [VMEM] * 9,
        [
            SMEM(wavelet.shape, f32), pltpu.SemaphoreType.DMA,
            VMEM((near * width, 3 * LANES), jnp.bfloat16), field, field,
        ],
        15 * ITERS * 2 * cells, 80 * cells,
    )
    rows = depth * width // shots
    both = VMEM((2, width, LANES), f32)
    field = VMEM((near, width + 2 * GUARD, LANES), f32)
    a, a_later, a_edge, b_edge, *pieces = call(
        functools.partial(adjoint_kernel, depth, width, shots),
        [own, own, both, both] + [VMEM((rows, LANES), f32)] * shots,
        (a0, a1, ga, gb, mod, weight, laps, extra, ua_edge, ub_edge), [VMEM] * 10,
        [VMEM((depth * width, LANES), f32), field, field],
        18 * ITERS * 2 * cells, 80 * cells,
    )

    def with_others(own_one, pieces, axis, order=far_first):
        got, perms = {}, partner_perms(lax.axis_size(axis))
        for m in order(len(perms) + 1):
            got[m] = lax.ppermute(pieces[m], axis, perms[m])
        return [own_one] + [got[m] for m in sorted(got)]

    parts = with_others(pieces[0], pieces, "shot")
    a_edge, b_edge = exchange(a_edge, b_edge)
    tile = VMEM((8, LANES), f32)
    grad, top = call(
        sum_kernel, [VMEM((rows, LANES), f32), tile], parts, [VMEM] * shots, [],
        shots * rows * LANES, 4 * shots * rows * LANES,
    )
    tops = with_others(top, [top] * slabs, "slab", lambda count: range(count - 1, 0, -1))
    (grad,) = call(
        top_kernel, [VMEM((rows + 8, LANES), f32)], [grad, *tops], [VMEM] * (slabs + 1), [],
        0, 4096 * shots,
    )
    grads = with_others(grad, [grad] * shots, "shot")
    pad = VMEM((depth + 2, width + 2 * GUARD, LANES), f32)
    base, lap, a = call(
        functools.partial(last_kernel, depth, width), [own, own, out],
        (u, u_later, a, a_later, a_edge, b_edge, mod, weight, extra), [VMEM] * 9,
        [pad, pad], 30 * cells, 32 * cells,
    )
    new_model, stepped = call(
        functools.partial(update_kernel, depth, width, shots), [out, out],
        (*grads, model, base, lap), [VMEM] * (shots + 3),
        [VMEM((depth * width, LANES), f32)], 10 * cells, 4 * 6 * cells,
    )
    return new_model, stepped[None], a[None]


def solution(mesh):
    in_specs = (
        P(("groups", "slab"), None, None),
        P(("groups", "shot"), "slab", None, None),
        P(("groups", "shot"), "slab", None, None),
        P(("groups", "shot"), "slab", None, None),
        P(("groups", "shot"), "slab", None, None),
        P(("groups", "shot"), None),
        P(("groups", "shot"), None, None),
        P(("groups", "shot")),
        P(("groups", "shot"), None),
    )
    out_specs = (
        P(("groups", "slab"), None, None),
        P(("groups", "shot"), "slab", None, None),
        P(("groups", "shot"), "slab", None, None),
    )
    return jax.shard_map(per_device, mesh=mesh, in_specs=in_specs, out_specs=out_specs, check_vma=False)
```

```python
import functools

import jax
import jax.numpy as jnp
from jax import lax
from jax.experimental import pallas as pl
from jax.experimental.pallas import tpu as pltpu
from jax.sharding import PartitionSpec as P


ITERS = 8
REACH = ITERS
GUARD = 8
LANES = 128
LIMIT = 16 * 2**20
VMEM = pltpu.VMEM
SMEM = pltpu.SMEM
HBM = pl.ANY


def pairs(count, start):
    low = [(i, i + 1) for i in range(start, count - 1, 2)]
    return low + [(b, a) for a, b in low]


def partner_perms(count):
    if count & (count - 1) == 0:
        return {m: [(i, i ^ m) for i in range(count)] for m in range(1, count)}
    return {m: [(i, (i + m) % count) for i in range(count)] for m in range(1, count)}


def far_first(count):
    half = count // 2
    return [*range(half, count), *range(1, half)]


def send_slot(me, m, count):
    return me ^ m if count & (count - 1) == 0 else lax.rem(me + m, count)


def from_slot(me, m, count):
    return me ^ m if count & (count - 1) == 0 else lax.rem(me - m + count, count)


def spec(space):
    return pl.BlockSpec(memory_space=space)


def cost(flops, nbytes):
    return pl.CostEstimate(flops=int(flops), bytes_accessed=int(nbytes), transcendentals=0)


def is_even():
    return lax.rem(lax.axis_index("slab"), 2) == 0


def pack_kernel(depth, sizes, *refs):
    count = (len(refs) - 4) // 2
    args, (to_a, to_b), whole, (sem, own_sem) = (
        refs[:count], refs[count : count + 2], refs[count + 2 : -2], refs[-2:],
    )

    def copies(up_a, up_b):
        out = []
        for j, (dst, up) in enumerate(((to_a, up_a), (to_b, up_b))):
            at = 0
            for i, (field, size) in enumerate(zip(args, sizes)):
                out.append(
                    pltpu.make_async_copy(
                        field.at[pl.ds(depth - size if up else 0, size)],
                        dst.at[pl.ds(at, size)],
                        sem.at[j, i],
                    )
                )
                at += size
        return out

    even = is_even()

    @pl.when(even)
    def _():
        for c in copies(True, False):
            c.start()

    @pl.when(jnp.logical_not(even))
    def _():
        for c in copies(False, True):
            c.start()

    own = [
        pltpu.make_async_copy(src, dst, own_sem.at[i]) for i, (src, dst) in enumerate(zip(args, whole))
    ]
    for c in own:
        c.start()
    for c in copies(False, False) + own:
        c.wait()


def hot_rows(base, rec_ref, left):
    index = rec_ref[...]
    row_of = index // LANES
    lane_of = index - row_of * LANES
    row_of = row_of - base
    group = 128
    for first in range(0, left.shape[0], group):
        at = lax.broadcasted_iota(jnp.int32, (group, LANES), 0) + first
        hot = jnp.where(at == row_of, 1.0, 0.0).astype(jnp.bfloat16)
        for part in range(3):
            left[pl.ds(first, group), pl.ds(part * LANES, LANES)] = hot
    return lane_of


def residuals(left, first, size, lane_of, value):
    mine = lax.broadcasted_iota(jnp.int32, (LANES, LANES), 0) == lane_of
    parts = []
    for _ in range(3):
        piece = value.astype(jnp.bfloat16).astype(jnp.float32)
        value = value - piece
        parts.append(jnp.where(mine, piece, 0.0).astype(jnp.bfloat16))
    return lax.dot_general(
        left[pl.ds(first, size), :], jnp.concatenate(parts, axis=1),
        (((1,), (1,)), ((), ())), preferred_element_type=jnp.float32,
    )


def around(src, p, width, first, last):
    starts = range(GUARD, GUARD + width, 8)
    here = [src[p, pl.ds(r, 8), :] for r in starts]
    after = [pltpu.roll(c, LANES - 1, 1) for c in here]
    before = [pltpu.roll(c, 1, 1) for c in here]
    out = []
    for r, c, x, y in zip(starts, here, after, before):
        s = src[p + 1, pl.ds(r, 8), :] + src[p - 1, pl.ds(r, 8), :]
        s = s + src[p, pl.ds(r + 1, 8), :]
        s = s + src[p, pl.ds(r - 1, 8), :]
        s = s + jnp.where(last, 0.0, x)
        s = s + jnp.where(first, 0.0, y)
        out.append((r - GUARD, c, s))
    return out


def edges():
    lane = lax.broadcasted_iota(jnp.int32, (8, LANES), 1)
    return lane == 0, lane == LANES - 1


def clear_guards(field):
    planes, rows, _ = field.shape
    zero = jnp.zeros((GUARD, LANES), jnp.float32)
    for p in range(planes):
        field[p, pl.ds(0, GUARD), :] = zero
        field[p, pl.ds(rows - GUARD, GUARD), :] = zero


def fill(depth, width, reach, own, a_in, b_in, bufs):
    rows = [pl.ds(GUARD if buf.shape[1] > width else 0, width) for buf in bufs]
    for src, buf, r in zip(own, bufs, rows):
        for p in range(depth):
            buf[reach + p, r, :] = src[p]

    def put(low, high):
        for buf, r, (lo, at, size), (hi, _, _) in zip(bufs, rows, low, high):
            for p in range(size):
                buf[reach - size + p, r, :] = lo[at + p]
                buf[reach + depth + p, r, :] = hi[at + p]

    even = is_even()

    @pl.when(even)
    def _():
        put(b_in, a_in)

    @pl.when(jnp.logical_not(even))
    def _():
        put(a_in, b_in)


def forward_kernel(
    depth, width, wavelet, src_index, rec_index, misfit, now, later, model, ua_in, ub_in, ha_in, hb_in,
    u_out, later_out, lap_out, a_edge, b_edge, mod, weight, extra,
    amplitude, sem, left, cur, old,
):
    n = REACH - 1
    slab = lax.axis_index("slab")
    fetch = pltpu.make_async_copy(wavelet, amplitude, sem)
    fetch.start()
    clear_guards(cur)
    clear_guards(old)
    fill(
        depth, width, REACH, (now, later, model),
        ((ua_in, 0, REACH), (ha_in, 0, n), (ha_in, n, n)),
        ((ub_in, 0, REACH), (hb_in, 0, n), (hb_in, n, n)),
        (cur, old, mod),
    )
    lane_of = hot_rows((slab * depth - n) * width, rec_index, left)
    fetch.wait()
    for p in range(1, depth + 2 * REACH - 1):
        weight[p] = 2.0 - 6.0 * mod[p]
    first, last = edges()
    source = src_index[0]
    src_row = source // LANES
    src_lane = source - src_row * LANES
    src_row = src_row - (slab * depth - REACH) * width
    bufs = (cur, old)
    for k in range(ITERS):
        s, d = bufs[k % 2], bufs[(k + 1) % 2]
        low, high = (k + 1, depth + 2 * n - 1 - k) if k < n else (n, n + depth)
        extra[k, pl.ds(low * width, (high - low) * width), :] = residuals(
            left, low * width, (high - low) * width, lane_of, misfit[pl.ds(k, 1), :]
        )
        for p in range(k + 1, depth + 2 * REACH - 1 - k):
            for r, c, total in around(s, p, width, first, last):
                lap = total - 6.0 * c
                here = (p, pl.ds(GUARD + r, 8), slice(None))
                d[here] = 2.0 * c - d[here] + mod[p, pl.ds(r, 8), :] * lap
                if REACH <= p < REACH + depth:
                    lap_out[k, p - REACH, pl.ds(r, 8), :] = lap

        @pl.when((src_row >= (k + 1) * width) & (src_row < (depth + 2 * REACH - 1 - k) * width))
        def _():
            plane = src_row // width
            here = (plane, pl.ds(GUARD + src_row - plane * width, 1), slice(None))
            at = lax.broadcasted_iota(jnp.int32, (1, LANES), 1) == src_lane
            d[here] = d[here] + jnp.where(at, amplitude[0, k], 0.0)

    u, u_later = bufs[ITERS % 2], bufs[(ITERS + 1) % 2]
    rows = pl.ds(GUARD, width)
    even = is_even()
    a_edge[...] = u[jnp.where(even, REACH + depth - 1, REACH), rows, :]
    b_edge[...] = u[jnp.where(even, REACH, REACH + depth - 1), rows, :]
    for p in range(depth):
        u_out[p] = u[REACH + p, rows, :]
        later_out[p] = u_later[REACH + p, rows, :]


def adjoint_kernel(
    depth, width, shots, now, later, a_in, b_in, mod, weight, laps, extra, ua_edge, ub_edge,
    a_out, later_out, a_edge, b_edge, *rest
):
    *pieces, image, cur, old = rest
    n = REACH - 1
    clear_guards(cur)
    clear_guards(old)
    fill(
        depth, width, n, (now, later),
        ((a_in, 0, n), (a_in, n, n - 1)), ((b_in, 0, n), (b_in, n, n - 1)),
        (cur, old),
    )
    first, last = edges()
    bufs = (cur, old)

    def imaged(k, p, r, c):
        into = pl.ds((p - n) * width + r, 8)
        add = c * laps[k, p - n, pl.ds(r, 8), :]
        image[into, :] = image[into, :] + add if k > 0 else add

    for k in range(n):
        s, d = bufs[k % 2], bufs[(k + 1) % 2]
        for p in range(k + 1, depth + 2 * n - 1 - k):
            for r, c, total in around(s, p, width, first, last):
                here = (p, pl.ds(GUARD + r, 8), slice(None))
                rows = pl.ds(r, 8)
                new = weight[p + 1, rows, :] * c - d[here] + mod[p + 1, rows, :] * total
                d[here] = new + extra[k, pl.ds(p * width + r, 8), :]
                if n <= p < n + depth:
                    imaged(k, p, r, c)

    a, a_later = bufs[n % 2], bufs[(n + 1) % 2]
    for p in range(n, n + depth):
        for r in range(0, width, 8):
            imaged(n, p, r, a[p, pl.ds(GUARD + r, 8), :])
    size = depth * width // shots
    me = lax.axis_index("shot")
    for m in range(shots):
        to = me if m == 0 else send_slot(me, m, shots)
        pieces[m][...] = image[pl.ds(pl.multiple_of(to * size, size), size), :]
    rows = pl.ds(GUARD, width)
    for p in range(depth):
        a_out[p] = a[n + p, rows, :]
        later_out[p] = a_later[n + p, rows, :]
    even = is_even()
    a_edge[0] = ua_edge[...]
    b_edge[0] = ub_edge[...]
    a_edge[1] = a[jnp.where(even, n + depth - 1, n), rows, :]
    b_edge[1] = a[jnp.where(even, n, n + depth - 1), rows, :]


def last_kernel(
    depth, width, u, u_later, a, a_later, a_in, b_in, mod, weight, extra,
    base_out, lap_out, adjoint_out,
    upad, apad,
):
    n = REACH - 1
    clear_guards(upad)
    clear_guards(apad)
    fill(
        depth, width, 1, (u, a), ((a_in, 0, 1), (a_in, 1, 1)), ((b_in, 0, 1), (b_in, 1, 1)),
        (upad, apad),
    )
    first, last = edges()
    for p in range(depth):
        for r, c, total in around(upad, p + 1, width, first, last):
            rows = pl.ds(r, 8)
            lap_out[p, rows, :] = total - 6.0 * c
            base_out[p, rows, :] = 2.0 * c - u_later[p, rows, :]
        for r, c, total in around(apad, p + 1, width, first, last):
            rows = pl.ds(r, 8)
            q = REACH + p
            new = weight[q, rows, :] * c - a_later[p, rows, :] + mod[q, rows, :] * total
            adjoint_out[p, rows, :] = new + extra[n, pl.ds((n + p) * width + r, 8), :]


def sum_kernel(*refs):
    *parts, out, top_out = refs
    top = jnp.zeros((8, LANES), jnp.float32)
    for r in range(0, out.shape[0], 8):
        total = parts[0][pl.ds(r, 8), :]
        for part in parts[1:]:
            total = total + part[pl.ds(r, 8), :]
        out[pl.ds(r, 8), :] = total
        top = jnp.maximum(top, jnp.abs(total))
    top_out[...] = top


def top_kernel(grad, *refs):
    *parts, out = refs
    n = grad.shape[0]
    out[pl.ds(0, n), :] = grad[...]
    top = parts[0][...]
    for part in parts[1:]:
        top = jnp.maximum(top, part[...])
    out[pl.ds(n, 8), :] = top


def update_kernel(depth, width, shots, *refs):
    grads, refs = refs[:shots], refs[shots:]
    model, base, laps, model_out, stepped_out, grad, new_model, stepped, sem = refs
    sent = []
    n = depth * width // shots
    me = lax.axis_index("shot")
    for m in range(shots):
        owner = me if m == 0 else from_slot(me, m, shots)
        grad[pl.ds(pl.multiple_of(owner * n, n), n), :] = grads[m][pl.ds(0, n), :]
    top = grads[0][pl.ds(n, 8), :]
    for other in grads[1:]:
        top = jnp.maximum(top, other[pl.ds(n, 8), :])
    peak = jnp.max(top)
    for p in range(depth):
        for r in range(0, width, 8):
            g = grad[pl.ds(p * width + r, 8), :]
            rows = pl.ds(r, 8)
            new = jnp.clip(model[p, rows, :] - 0.1 * g / (peak + 1e-06), 0.05, 0.3)
            new_model[p, rows, :] = new
            stepped[p, rows, :] = base[p, rows, :] + new * laps[p, rows, :]
        for i, (src, dst) in enumerate(((new_model, model_out), (stepped, stepped_out))):
            sent.append(pltpu.make_async_copy(src.at[p], dst.at[p], sem.at[i, p]))
            sent[-1].start()
    for copy in sent:
        copy.wait()


def placed(x, space):
    if space is VMEM or space is pltpu.HBM:
        return pltpu.with_memory_space_constraint(x, space)
    return x


def call(kernel, outs, args, spaces, scratch, flops, nbytes, out_space=VMEM):
    args = [placed(x, space) for x, space in zip(args, spaces)]
    return pl.pallas_call(
        kernel,
        out_shape=outs,
        in_specs=[spec(space) for space in spaces],
        out_specs=[spec(out_space)] * len(outs),
        scratch_shapes=scratch,
        cost_estimate=cost(flops, nbytes),
        compiler_params=pltpu.CompilerParams(vmem_limit_bytes=LIMIT),
    )(*args)


def per_device(model, fwd_now, fwd_next, adj_now, adj_next, wavelet, misfit, src_index, rec_index):
    f32 = jnp.float32
    depth, width, length = model.shape
    assert length == LANES and fwd_now.shape[0] == 1 and width % 8 == 0 and depth == REACH
    u0, u1, a0, a1 = fwd_now[0], fwd_next[0], adj_now[0], adj_next[0]
    slabs, shots = lax.axis_size("slab"), lax.axis_size("shot")
    perm_a, perm_b = pairs(slabs, 0), pairs(slabs, 1)
    planes = depth + 2 * REACH
    cells = depth * width * LANES
    own = VMEM((depth, width, LANES), f32)
    wide = VMEM((planes, width, LANES), f32)
    field = VMEM((planes, width + 2 * GUARD, LANES), f32)
    edge = VMEM((width, LANES), f32)
    out = jax.ShapeDtypeStruct((depth, width, LANES), f32)
    n = REACH - 1

    def exchange(to_a, to_b):
        b = lax.ppermute(to_b, "slab", perm_b)
        return lax.ppermute(to_a, "slab", perm_a), b

    def packed(args, sizes):
        total = sum(sizes)
        to_a, to_b, *whole = call(
            functools.partial(pack_kernel, depth, sizes),
            [VMEM((total, width, LANES), f32)] * 2 + [VMEM(x.shape, x.dtype) for x in args],
            args, [pltpu.HBM] * len(args),
            [pltpu.SemaphoreType.DMA((2, len(sizes))), pltpu.SemaphoreType.DMA((len(args),))],
            0, 4 * 4 * total * width * LANES,
        )
        return (to_a, to_b), whole

    ua, ub = exchange(u0, u0)
    to, (u1, model, u0) = packed((u1, model, u0), (n, n))
    ha, hb = exchange(*to)
    to, (a0, a1, rec_index, misfit) = packed((a0, a1, rec_index, misfit[0]), (n, n - 1))
    ga, gb = exchange(*to)
    near = depth + 2 * n
    u, u_later, laps, ua_edge, ub_edge, mod, weight, extra = call(
        functools.partial(forward_kernel, depth, width),
        [
            own, own, VMEM((ITERS, depth, width, LANES), f32), edge, edge, wide, wide,
            VMEM((ITERS, near * width, LANES), f32),
        ],
        (wavelet, src_index, rec_index, misfit, u0, u1, model, ua, ub, ha, hb),
        [pltpu.HBM, SMEM] + [VMEM] * 9,
        [
            SMEM(wavelet.shape, f32), pltpu.SemaphoreType.DMA,
            VMEM((near * width, 3 * LANES), jnp.bfloat16), field, field,
        ],
        15 * ITERS * 2 * cells, 80 * cells,
    )
    rows = depth * width // shots
    both = VMEM((2, width, LANES), f32)
    field = VMEM((near, width + 2 * GUARD, LANES), f32)
    a, a_later, a_edge, b_edge, *pieces = call(
        functools.partial(adjoint_kernel, depth, width, shots),
        [own, own, both, both] + [VMEM((rows, LANES), f32)] * shots,
        (a0, a1, ga, gb, mod, weight, laps, extra, ua_edge, ub_edge), [VMEM] * 10,
        [VMEM((depth * width, LANES), f32), field, field],
        18 * ITERS * 2 * cells, 80 * cells,
    )

    def with_others(own_one, pieces, axis, order=far_first):
        got, perms = {}, partner_perms(lax.axis_size(axis))
        for m in order(len(perms) + 1):
            got[m] = lax.ppermute(pieces[m], axis, perms[m])
        return [own_one] + [got[m] for m in sorted(got)]

    parts = with_others(pieces[0], pieces, "shot")
    a_edge, b_edge = exchange(a_edge, b_edge)
    tile = VMEM((8, LANES), f32)
    grad, top = call(
        sum_kernel, [VMEM((rows, LANES), f32), tile], parts, [VMEM] * shots, [],
        shots * rows * LANES, 4 * shots * rows * LANES,
    )
    tops = with_others(top, [top] * slabs, "slab", lambda count: range(count - 1, 0, -1))
    (grad,) = call(
        top_kernel, [VMEM((rows + 8, LANES), f32)], [grad, *tops], [VMEM] * (slabs + 1), [],
        0, 4096 * shots,
    )
    grads = with_others(grad, [grad] * shots, "shot")
    pad = VMEM((depth + 2, width + 2 * GUARD, LANES), f32)
    base, lap, a = call(
        functools.partial(last_kernel, depth, width), [own, own, out],
        (u, u_later, a, a_later, a_edge, b_edge, mod, weight, extra), [VMEM] * 9,
        [pad, pad], 30 * cells, 32 * cells,
    )
    new_model, stepped = call(
        functools.partial(update_kernel, depth, width, shots), [out, out],
        (*grads, model, base, lap), [VMEM] * (shots + 3),
        [VMEM((depth * width, LANES), f32), own, own, pltpu.SemaphoreType.DMA((2, depth))],
        10 * cells, 4 * 6 * cells, HBM,
    )
    return new_model, stepped[None], a[None]


def solution(mesh):
    in_specs = (
        P(("groups", "slab"), None, None),
        P(("groups", "shot"), "slab", None, None),
        P(("groups", "shot"), "slab", None, None),
        P(("groups", "shot"), "slab", None, None),
        P(("groups", "shot"), "slab", None, None),
        P(("groups", "shot"), None),
        P(("groups", "shot"), None, None),
        P(("groups", "shot")),
        P(("groups", "shot"), None),
    )
    out_specs = (
        P(("groups", "slab"), None, None),
        P(("groups", "shot"), "slab", None, None),
        P(("groups", "shot"), "slab", None, None),
    )
    return jax.shard_map(per_device, mesh=mesh, in_specs=in_specs, out_specs=out_specs, check_vma=False)
```
